32 devices in a mesh: expert: 4 (over y, core), dp: 8 (over z, x).
Axes of the slice: x: 2, y: 2, z: 4, core: 2. Of those that a mesh axis runs over, the one named last changes fastest.
Arguments:
- tokens: bfloat16 [4096, 1024], P(('expert', 'dp')), may hold values from -6 to 6
- d_output: bfloat16 [4096, 1024], P(('expert', 'dp')), may hold values from -6 to 6
- expert_ids: int32 [4096, 8], P(('expert', 'dp')), may hold values from 0 to 127, as said below
- gate_scores: bfloat16 [4096, 8], P(('expert', 'dp')), may hold values from 0.099609375 to 1
- gate_up_w: bfloat16 [4, 1024, 768], P('expert', 'dp'), may hold values from -0.1875 to 0.1875
- down_w: bfloat16 [4, 1024, 384], P('expert', 'dp'), may hold values from -0.3125 to 0.3125
Outputs:
- d_tokens: bfloat16 [4096, 1024], P(('expert', 'dp'))
- d_gates: bfloat16 [4096, 8], P(('expert', 'dp'))
- d_down: float32 [4, 1024, 384], P('expert', 'dp')
The draws below stay inside these ranges and needn't reach their ends.
Inputs may be any that keep to these rules, and one draw needn't show every extreme that they name: `expert_ids`: each token names 8 different experts. The tokens of one device name no expert more than 12 times, and in every draw one expert below 4 is named exactly 12 times by the tokens of every device.
All inputs are finite; a program needn't handle non-finite values.
Results may differ from the reference program's by a relative error of at most 0.0062.
Values may be sent and summed in bfloat16 or wider, within the bound.
A program may use at most 64 MiB of HBM per device.

```python
import math
import jax
import jax.numpy as jnp
from jax import lax

D = 1024
FF = 384
E_ALL = 128
TOPK = 8
TOK_DEV = 128
CAP = 12
EXPERTS = 4
TOKENS = 4096
N_EXPERT = 4
N_DP = 8


def draw_expert_ids(key, part):
    blocks = TOKENS // TOK_DEV
    mean_count = TOK_DEV * TOPK // E_ALL
    full_key, block_key = jax.random.split(jax.random.fold_in(key, 7311))
    heavy = jax.random.randint(full_key, (), 0, EXPERTS)
    block_keys = jax.random.split(block_key, blocks)

    def one_block(single_key):
        order_key, spread_key, column_key = jax.random.split(single_key, 3)
        order = jax.random.permutation(order_key, E_ALL).astype(jnp.int32)
        spread = jax.random.randint(spread_key, (E_ALL // 2,), 0, CAP - mean_count + 1)
        counts = jnp.zeros((E_ALL,), jnp.int32)
        counts = counts.at[order[0::2]].set(mean_count + spread)
        counts = counts.at[order[1::2]].set(mean_count - spread)
        position = jnp.sum(jnp.where(order == heavy, jnp.arange(E_ALL, dtype=jnp.int32), 0))
        partner = order[jnp.bitwise_xor(position, 1)]
        counts = counts.at[heavy].set(CAP).at[partner].set(2 * mean_count - CAP)
        running = jnp.cumsum(counts[order])
        places = jnp.arange(TOK_DEV * TOPK, dtype=jnp.int32)
        which = jnp.searchsorted(running, places, side='right').astype(jnp.int32)
        labels = order[which].reshape(TOPK, TOK_DEV)
        columns = jax.random.permutation(column_key, TOK_DEV)
        return labels.T[columns]
    return jax.vmap(one_block)(block_keys).reshape(TOKENS, TOPK).astype(jnp.int32)


def steps_of(stream_key, shape, cuts, low, top_value):
    factor_of, own = 1.0, jax.random.fold_in(stream_key, 6)
    for axis_at, shards_of in cuts:
        heights = jnp.exp(jax.random.uniform(jax.random.fold_in(own, axis_at), (shards_of,), jnp.float32, low / len(cuts), top_value / len(cuts)))
        factor_of = factor_of * jnp.repeat(heights, shape[axis_at] // shards_of).reshape([-1 if axis == axis_at else 1 for axis in range(len(shape))])
    return factor_of


def scatter_about(own_key, dims, scale, limit, cuts=(), kind=jnp.bfloat16):
    result = jax.random.normal(own_key, dims, jnp.float32) * scale
    if len(cuts) > 0:
        result = steps_of(own_key, dims, cuts, -0.22, 0.18) * result
    return jnp.clip(result, min=-limit, max=limit).astype(kind)


def setup_inputs(seed: int = 0) -> dict:
    key_list = jax.random.split(jax.random.key(seed), 7)
    return {
        "tokens": scatter_about(key_list[0], (TOKENS, D), 1.0, 6.0, ((0, 32),)),
        "d_output": scatter_about(key_list[1], (TOKENS, D), 1.0, 6.0, ((0, 32),)),
        "expert_ids": draw_expert_ids(jax.random.fold_in(key_list[6], 71), 0),
        "gate_scores": jnp.clip(jnp.exp(math.log(1.0) - 2.306499 * jax.random.uniform(key_list[3], (TOKENS, TOPK), jnp.float32) ** steps_of(key_list[3], (TOKENS, TOPK), ((0, 32),), -0.2, 0.2)), 0.099609375, 1.0).astype(jnp.bfloat16),
        "gate_up_w": scatter_about(key_list[4], (EXPERTS, D, 2 * FF), D ** -0.5, 0.1875, ((0, 4), (1, 8))),
        "down_w": scatter_about(key_list[5], (EXPERTS, D, FF), FF ** -0.5, 0.3125, ((0, 4), (1, 8))),
    }


def to_half(values):
    return lax.optimization_barrier(values.astype(jnp.bfloat16)).astype(jnp.float32)


def matmul(left, right):
    return jnp.dot(left, right, precision=lax.Precision.HIGHEST, preferred_element_type=jnp.float32)


def reference(tokens, d_output, expert_ids, gate_scores, gate_up_w, down_w):
    most_rows = CAP * N_EXPERT * N_DP
    total_tokens = tokens.shape[0]
    width = down_w.shape[2]

    def expert_step(carry, expert):
        grad_tokens, grad_gates = carry
        chosen = expert_ids == expert
        picked = jnp.any(chosen, axis=1)
        row_index = jnp.nonzero(picked, size=most_rows, fill_value=0)[0].astype(jnp.int32)
        alive = (jnp.arange(most_rows) < jnp.sum(picked.astype(jnp.int32))).astype(jnp.float32)
        chosen_rows = chosen[row_index]
        inputs = tokens[row_index].astype(jnp.float32)
        upstream = d_output[row_index].astype(jnp.float32)
        gate_rows = jnp.sum(jnp.where(chosen_rows, gate_scores[row_index].astype(jnp.float32), 0.0), axis=1) * alive
        weight_gu = gate_up_w[expert].astype(jnp.float32)
        weight_down = down_w[expert].astype(jnp.float32)
        pre_act = matmul(inputs, weight_gu)
        gate_part = pre_act[:, :width]
        up_part = pre_act[:, width:]
        sigma = jax.nn.sigmoid(gate_part)
        activ = gate_part * sigma
        hidden = to_half(activ * up_part)
        expert_out = matmul(hidden, weight_down.T)
        slot_grad = to_half(jnp.sum(upstream * expert_out, axis=1)) * alive
        d_expert_out = to_half(gate_rows[:, None] * upstream)
        d_hidden = matmul(d_expert_out, weight_down)
        d_gate_part = d_hidden * up_part * sigma * (1.0 + gate_part * (1.0 - sigma))
        d_up_part = d_hidden * activ
        d_pre = to_half(jnp.concatenate([d_gate_part, d_up_part], axis=1))
        d_slot = to_half(matmul(d_pre, weight_gu.T)) * alive[:, None]
        grad_down = matmul(d_expert_out.T, hidden)
        grad_tokens = grad_tokens.at[row_index].add(d_slot)
        grad_gates = grad_gates.at[row_index].add(jnp.where(chosen_rows, slot_grad[:, None], 0.0))
        return (grad_tokens, grad_gates), grad_down

    start = (jnp.zeros((total_tokens, tokens.shape[1]), jnp.float32), jnp.zeros(expert_ids.shape, jnp.float32))
    (grad_tokens, grad_gates), grad_down = lax.scan(expert_step, start, jnp.arange(EXPERTS, dtype=jnp.int32))
    return grad_tokens.astype(jnp.bfloat16), grad_gates.astype(jnp.bfloat16), grad_down
```

```python
import functools

import jax
import jax.numpy as jnp
from jax import lax
from jax.experimental import pallas as pl
from jax.experimental.pallas import tpu as pltpu
from jax.sharding import PartitionSpec as P

CAP = 12
PAD = 16
LANES = 128
BF = jnp.bfloat16
F32 = jnp.float32


def dot(left, right, dims=((1,), (0,))):
    return lax.dot_general(left, right, (dims, ((), ())), preferred_element_type=F32)


def ring_kernel(groups, outer, inner, tok, dout, ids, scores, gate_in, down_in,
           o_tok, o_gates, o_down,
           gate_buf, down_buf, x_ch, up_ch, pre_acc, u_acc, send, recv, hid_buf, dx_send, dx_buf, ret, back,
           w_send, w_recv, own_sem, s_send, s_recv, h_send, h_recv, x_send, x_recv, b_send, b_recv):
    n = outer * inner
    me = lax.axis_index("dp")
    mine = lax.axis_index("expert")
    zo = me // inner
    xi = me - zo * inner
    slots = groups * PAD
    rows = gate_in.shape[1]
    feats = tok.shape[1]
    width = down_in.shape[2]
    ins = (down_in, gate_in)
    bufs = (down_buf, gate_buf)

    barrier = pltpu.get_barrier_semaphore()
    for k in range(1, n):
        pl.semaphore_signal(barrier, inc=1, device_id={"dp": lax.rem(me + k, n)},
                            device_id_type=pl.DeviceIdType.MESH)
    for k in range(1, groups):
        pl.semaphore_signal(barrier, inc=1, device_id={"expert": lax.rem(mine + k, groups)},
                            device_id_type=pl.DeviceIdType.MESH)
    pl.semaphore_wait(barrier, n - 1 + groups - 1)

    def remote(src, dst, ss, rs, **where):
        return pltpu.make_async_remote_copy(
            src_ref=src, dst_ref=dst, send_sem=ss, recv_sem=rs,
            device_id=where, device_id_type=pl.DeviceIdType.MESH)

    def target(way):
        return me + (inner, -inner, 1, -1)[way]

    def can(way):
        return (zo < outer - 1, zo > 0, xi < inner - 1, xi > 0)[way]

    def hop(w, s, way, own=False):
        src = ins[w].at[0] if own else bufs[w].at[s]
        return remote(src, bufs[w].at[s], w_send.at[w, way, s], w_recv.at[w, s], dp=target(way))

    started = []
    accs = (u_acc, pre_acc)
    chunks = (up_ch, x_ch)

    def forward(w, s, way, valid, own=False):
        ok = can(way) if valid is None else jnp.logical_and(can(way), valid)

        @pl.when(ok)
        def _():
            hop(w, s, way, own).start()
        started.append((ok, w, s, way, own))

    def arrive(w, s, valid):
        @pl.when(valid)
        def _():
            hop(w, s, 0).wait_recv()

    def add(w, s, valid):
        @pl.when(valid)
        def _():
            accs[w][...] += dot(chunks[w][s], bufs[w][s])

    def outer_shards(d):
        return ((0, me - d * inner, zo >= d), (1, me + d * inner, zo + d < outer))

    def outer_step(w, d):
        for way, s, valid in outer_shards(d):
            arrive(w, s, valid)
            for go in (way, 2, 3):
                forward(w, s, go, valid)

    def outer_add(w, d):
        for _, s, valid in outer_shards(d):
            add(w, s, valid)

    def inner_step(w, d):
        for di in range(1, inner):
            for sign in ((1,) if d == 0 else (-1, 1)):
                so = zo + sign * d
                good = jnp.logical_and(so >= 0, so < outer)
                for way, step in ((2, -di), (3, di)):
                    xs = xi + step
                    valid = jnp.logical_and(good, jnp.logical_and(xs >= 0, xs < inner))
                    s = so * inner + xs
                    arrive(w, s, valid)
                    if inner > 2:
                        forward(w, s, way, valid)
                    add(w, s, valid)

    own = [pltpu.make_async_copy(ins[w].at[0], bufs[w].at[me], own_sem.at[w]) for w in range(2)]
    for way in range(4):
        forward(1, me, way, None, own=True)
    for way in range(4):
        forward(0, me, way, None, own=True)
    for c in own:
        c.start()

    t_rows = tok.shape[0]
    topk = ids.shape[0]
    row = lax.broadcasted_iota(jnp.int32, (slots, t_rows), 0)
    row_e = row // PAD
    row_r = (row - row_e * PAD).astype(F32)
    idv = ids[...]
    scv = scores[...].astype(F32)
    live = jnp.zeros((slots, t_rows), F32)
    gcol = jnp.zeros((slots, t_rows), F32)
    hits = []
    for k in range(topk):
        hit = idv[k:k + 1, :] == row_e
        hits.append(hit)
        live = jnp.where(hit, 1.0, live)
        gcol = jnp.where(hit, scv[k:k + 1, :], gcol)
    upper = (lax.broadcasted_iota(jnp.int32, (t_rows, t_rows), 0)
             < lax.broadcasted_iota(jnp.int32, (t_rows, t_rows), 1))
    rank = dot(live.astype(BF), jnp.where(upper, 1.0, 0.0).astype(BF))
    pick_t = jnp.where(rank == row_r, live, 0.0)
    pick_b = pick_t.astype(BF)
    send[:, 2 * feats:] = jnp.broadcast_to(
        jnp.sum(pick_t * gcol, axis=1, keepdims=True), (slots, LANES)).astype(BF)
    send[:, :feats] = dot(pick_b, tok[...]).astype(BF)
    send[:, feats:2 * feats] = dot(pick_b, dout[...]).astype(BF)

    def block(e):
        return pl.ds(pl.multiple_of(e * PAD, PAD), PAD)

    def swap(src, dst, ss, rs, k):
        e = lax.rem(mine + k, groups)
        return remote(src.at[block(e), :], dst.at[block(mine), :], ss.at[k], rs.at[k], expert=e)

    for k in range(1, groups):
        swap(send, recv, s_send, s_recv, k).start()
    recv[block(mine), :] = send[block(mine), :]
    pick = jnp.transpose(pick_t).astype(BF)

    def peer(src, dst, ss, rs, k, sliced):
        d = lax.rem(me + k, n)
        return remote(src.at[d] if sliced else src.at[me], dst.at[me], ss.at[k], rs.at[k], dp=d)

    if outer > 1:
        outer_step(1, 1)
        outer_step(0, 1)

    packed = groups * CAP
    pr = lax.broadcasted_iota(jnp.int32, (packed, slots), 0)
    pc = lax.broadcasted_iota(jnp.int32, (packed, slots), 1)
    pack = jnp.where(pc == (pr // CAP) * PAD + pr % CAP, 1.0, 0.0).astype(BF)

    for k in range(1, groups):
        swap(send, recv, s_send, s_recv, k).wait_recv()
    gates = recv[:, 2 * feats:2 * feats + 1].astype(F32)
    upstream = recv[:, feats:2 * feats]
    dexp = dot(pack, (gates * upstream.astype(F32)).astype(BF)).astype(BF)
    for d in range(n):
        dx_send[d] = dexp[:, d * rows:(d + 1) * rows]
        x_ch[d] = recv[:, d * rows:(d + 1) * rows]
        up_ch[d] = recv[:, feats + d * rows:feats + (d + 1) * rows]
    for k in range(1, n):
        peer(dx_send, dx_buf, x_send, x_recv, k, True).start()
    dx_buf[me] = dx_send[me]
    pre_acc[...] = dot(x_ch[me], gate_in[0])
    u_acc[...] = dot(up_ch[me], down_in[0])

    for d in range(2, outer):
        outer_step(1, d)
        outer_step(0, d)
        outer_add(1, d - 1)
        outer_add(0, d - 1)
    for d in range(outer - 1):
        inner_step(1, d)
        inner_step(0, d)
    if outer > 1:
        outer_add(1, outer - 1)
        outer_add(0, outer - 1)
    inner_step(1, outer - 1)

    pre = pre_acc[...]
    a = pre[:, :width]
    b = pre[:, width:]
    sig = jax.nn.sigmoid(a)
    act = a * sig
    hidden = (act * b).astype(BF)
    hid_buf[me] = dot(pack, hidden).astype(BF)
    for k in range(1, n):
        peer(hid_buf, hid_buf, h_send, h_recv, k, False).start()

    inner_step(0, outer - 1)
    for c in own:
        c.wait()

    u = u_acc[...]
    d_hid = gates * u
    d_pre = jnp.concatenate(
        [d_hid * b * sig * (1.0 + a * (1.0 - sig)), d_hid * act], axis=1).astype(BF)
    gate_full = gate_buf[...].reshape(n * rows, 2 * width)
    ret[:, feats:] = jnp.broadcast_to(
        jnp.sum(hidden.astype(F32) * u, axis=1, keepdims=True), (slots, LANES)).astype(BF)
    ret[:, :feats] = dot(d_pre, gate_full, ((1,), (1,))).astype(BF)
    for k in range(1, groups):
        swap(ret, back, b_send, b_recv, k).start()
    back[block(mine), :] = ret[block(mine), :]

    o_down[0] = dot(dx_buf[me], hid_buf[me], ((0,), (0,)))
    for k in range(1, n):
        s = lax.rem(me - k + n, n)
        peer(dx_send, dx_buf, x_send, x_recv, k, True).wait_recv()
        peer(hid_buf, hid_buf, h_send, h_recv, k, False).wait_recv()
        o_down[0] += dot(dx_buf[s], hid_buf[s], ((0,), (0,)))

    for k in range(1, groups):
        swap(ret, back, b_send, b_recv, k).wait_recv()
    o_tok[...] = dot(pick, back[:, :feats]).astype(BF)
    weighted = pick_t * back[:, feats:feats + 1].astype(F32)
    o_gates[...] = jnp.concatenate(
        [jnp.sum(jnp.where(hit, weighted, 0.0), axis=0, keepdims=True) for hit in hits],
        axis=0).astype(BF)

    for ok, w, s, way, is_own in started:
        @pl.when(ok)
        def _(w=w, s=s, way=way, is_own=is_own):
            hop(w, s, way, is_own).wait_send()
    for k in range(1, groups):
        swap(send, recv, s_send, s_recv, k).wait_send()
        swap(ret, back, b_send, b_recv, k).wait_send()
    for k in range(1, n):
        peer(dx_send, dx_buf, x_send, x_recv, k, True).wait_send()
        peer(hid_buf, hid_buf, h_send, h_recv, k, False).wait_send()

def remote(src, dst, ss, rs, **where):
    return pltpu.make_async_remote_copy(
        src_ref=src, dst_ref=dst, send_sem=ss, recv_sem=rs,
        device_id=where, device_id_type=pl.DeviceIdType.MESH)


def mid_kernel(groups, gate_in, down_in, tok_in, dout_in, ids_in, sc_in,
               o_tok, o_gates, o_down,
               gate_buf, down_buf, tok_v, dout_v, ids_v, sc_v, send, recv, pre_acc, v_acc,
               dx_send, dx_buf, hid_buf, ret, back,
               l_sem, w_send, w_recv, s_send, s_recv, x_send, x_recv,
               h_send, h_recv, b_send, b_recv):
    me = lax.axis_index("dp")
    mine = lax.axis_index("expert")
    zo = me // 2
    xi = me - 2 * zo
    side = zo // 2
    mid = jnp.logical_or(zo == 1, zo == 2)
    end = jnp.logical_not(mid)
    slots = groups * PAD
    rows = gate_in.shape[1]
    half = rows // 2
    feats = tok_in.shape[1]
    width = down_in.shape[2]
    n = feats // rows

    def at(x, z):
        return 2 * z + x

    xo = 1 - xi
    pal = at(xo, zo)
    z_mid, z_end, z_far, z_edge = 1 + side, 3 * side, 2 - side, 3 - 3 * side
    my_mid, my_end = at(xi, z_mid), at(xi, z_end)
    far_mid, far_end = at(xi, z_far), at(xi, z_edge)
    line = jnp.where(mid, far_mid, my_mid)

    barrier = pltpu.get_barrier_semaphore()

    def greet(**where):
        pl.semaphore_signal(barrier, inc=1, device_id=where, device_id_type=pl.DeviceIdType.MESH)

    greet(dp=pal)

    @pl.when(end)
    def _():
        for e in range(groups):
            greet(dp=my_mid, expert=e)

    @pl.when(mid)
    def _():
        greet(dp=far_mid)
        for e in range(groups):
            greet(dp=my_end, expert=e)
        for k in range(1, groups):
            greet(expert=lax.rem(mine + k, groups))

    local = [pltpu.make_async_copy(src, dst, l_sem.at[i]) for i, (src, dst) in enumerate((
        (ids_in, ids_v), (sc_in, sc_v), (tok_in, tok_v), (dout_in, dout_v),
        (gate_in.at[0], gate_buf.at[me]), (down_in.at[0], down_buf.at[me])))]
    for c in local:
        c.start()
    pl.semaphore_wait(barrier, 1 + groups * (1 + mid.astype(jnp.int32)))

    def piece(s, p, way, own=False):
        if p < 2:
            part = pl.ds(p * half, half)
            src = gate_in.at[0, part] if own else gate_buf.at[s, part]
            dst = gate_buf.at[s, part]
        else:
            src = down_in.at[0] if own else down_buf.at[s]
            dst = down_buf.at[s]
        return remote(src, dst, w_send.at[way, s, p], w_recv.at[s, p], dp=(line, pal)[way])

    def own_out(p):
        piece(me, p, 0, True).start()
        piece(me, p, 1, True).start()

    def take(s, p, *out):
        piece(s, p, 0).wait_recv()
        for way in out:
            piece(s, p, way).start()

    own_out(0)
    own_out(1)

    for c in local[:4]:
        c.wait()
    t_rows = tok_v.shape[0]
    topk = ids_v.shape[0]
    row = lax.broadcasted_iota(jnp.int32, (slots, t_rows), 0)
    row_e = row // PAD
    row_r = (row - row_e * PAD).astype(F32)
    idv = ids_v[...]
    scv = sc_v[...].astype(F32)
    live = jnp.zeros((slots, t_rows), F32)
    gcol = jnp.zeros((slots, t_rows), F32)
    hits = []
    for k in range(topk):
        hit = idv[k:k + 1, :] == row_e
        hits.append(hit)
        live = jnp.where(hit, 1.0, live)
        gcol = jnp.where(hit, scv[k:k + 1, :], gcol)
    upper = (lax.broadcasted_iota(jnp.int32, (t_rows, t_rows), 0)
             < lax.broadcasted_iota(jnp.int32, (t_rows, t_rows), 1))
    rank = dot(live.astype(BF), jnp.where(upper, 1.0, 0.0).astype(BF))
    pick_t = jnp.where(rank == row_r, live, 0.0)
    pick_b = pick_t.astype(BF)
    gate_col = jnp.sum(pick_t * gcol, axis=1, keepdims=True)
    send[:, 2 * feats:] = jnp.broadcast_to(gate_col, (slots, LANES)).astype(BF)
    send[:, :feats] = dot(pick_b, tok_v[...]).astype(BF)
    send[:, feats:2 * feats] = (gate_col * dot(pick_b, dout_v[...])).astype(BF)

    def block(i):
        start = i * PAD
        return pl.ds(start if isinstance(i, int) else pl.multiple_of(start, PAD), PAD)

    def slots_to(e, place):
        return remote(send.at[block(e), :], recv.at[block(place * groups + mine), :],
                      s_send.at[e], s_recv.at[place, mine], dp=my_mid, expert=e)

    def slots_from(place, e):
        return remote(send.at[block(e), :], recv.at[block(place * groups + e), :],
                      s_send.at[e], s_recv.at[place, e], dp=my_mid, expert=e)

    def other(k):
        return lax.rem(mine + k, groups)

    @pl.when(end)
    def _():
        for e in range(groups):
            slots_to(e, 1).start()
        take(pal, 0, 0)
        take(pal, 1, 0)
        own_out(2)
        take(pal, 2, 0)

    @pl.when(mid)
    def _():
        for k in range(1, groups):
            slots_to(other(k), 0).start()
        recv[block(mine), :] = send[block(mine), :]

    pick = jnp.transpose(pick_t).astype(BF)

    def dx_to(d):
        return remote(dx_send.at[d], dx_buf.at[2 * side + xi], x_send.at[d], x_recv.at[2 * side + xi], dp=d)

    def dx_from(q):
        return remote(dx_send.at[0], dx_buf.at[q], x_send.at[0], x_recv.at[q], dp=pal)

    def hid(q, d):
        return remote(hid_buf.at[q], hid_buf.at[q], h_send.at[q, d], h_recv.at[q], dp=d)

    def ret_to(place, e):
        return remote(ret.at[block(place * groups + e), :], back.at[block(mine), :],
                      b_send.at[place, e], b_recv.at[mine], dp=(my_mid, my_end)[place], expert=e)

    def back_from(e):
        return remote(ret.at[block(e), :], back.at[block(e), :],
                      b_send.at[0, e], b_recv.at[e], dp=my_mid, expert=e)

    my_q, pal_q = 2 * side + xi, 2 * side + xo
    far_q, fpal_q = 2 - 2 * side + xi, 2 - 2 * side + xo
    a, b, c, d, e_, f, g = (my_end, at(xo, z_end), pal, far_mid, far_end, at(xo, z_far), at(xo, z_edge))

    @pl.when(mid)
    def _():
        many = 2 * slots
        packed = 2 * groups * CAP

        def cols(base, s):
            return pl.ds(pl.multiple_of(base + s * rows, LANES), rows)

        def add(s):
            pre_acc[...] += dot(recv[:, cols(0, s)], gate_buf[s])

        def add_v(s):
            v_acc[...] += dot(recv[:, cols(feats, s)], down_buf[s])

        take(a, 0, 0)
        take(c, 0, 0)
        take(d, 0)
        take(a, 1, 0)
        take(c, 1)
        take(d, 1, 1)
        for k in range(1, groups):
            slots_from(0, other(k)).wait_recv()
        for e in range(groups):
            slots_from(1, e).wait_recv()
        pr = lax.broadcasted_iota(jnp.int32, (packed, many), 0)
        pc = lax.broadcasted_iota(jnp.int32, (packed, many), 1)
        pack = jnp.where(pc == (pr // CAP) * PAD + pr % CAP, 1.0, 0.0).astype(BF)
        dexp = dot(pack, recv[:, feats:2 * feats]).astype(BF)
        for s in range(n):
            dx_send[s] = dexp[:, s * rows:(s + 1) * rows]
        dx_buf[my_q] = dx_send[me]
        take(b, 0)
        take(e_, 0, 1)
        local[4].wait()
        pre_acc[...] = dot(recv[:, cols(0, me)], gate_buf[me])
        take(b, 1)
        take(e_, 1, 1)
        own_out(2)
        for s in (a, c, d):
            add(s)
        take(a, 2, 0)
        take(f, 0)
        take(f, 1)
        take(c, 2, 0)
        local[5].wait()
        v_acc[...] = dot(recv[:, cols(feats, me)], down_buf[me])
        for s in (b, e_, f):
            add(s)
        take(g, 0)
        take(g, 1)
        add(g)

        pre = pre_acc[...]
        ga = pre[:, :width]
        gb = pre[:, width:]
        sig = jax.nn.sigmoid(ga)
        act = ga * sig
        hidden = (act * gb).astype(BF)
        hid_buf[my_q] = dot(pack, hidden).astype(BF)
        for s in (far_end, far_mid, my_end, pal):
            hid(my_q, s).start()
        for s in (a, b, c, d, e_, f, g):
            dx_to(s).start()

        take(d, 2)
        for s in (a, c, d):
            add_v(s)
        take(b, 2)
        take(e_, 2, 1)
        for s in (b, e_):
            add_v(s)
        take(f, 2)
        add_v(f)
        take(g, 2)
        add_v(g)

        d_hid = v_acc[...]
        d_pre = jnp.concatenate(
            [d_hid * gb * sig * (1.0 + ga * (1.0 - sig)), d_hid * act], axis=1).astype(BF)
        gate_full = gate_buf[...].reshape(n * rows, 2 * width)
        gates = recv[:, 2 * feats:2 * feats + 1].astype(F32)
        inverse = jnp.where(gates > 0.0, 1.0 / jnp.where(gates > 0.0, gates, 1.0), 0.0)
        slot_grad = jnp.sum(hidden.astype(F32) * d_hid, axis=1, keepdims=True) * inverse
        ret[:, feats:] = jnp.broadcast_to(slot_grad, (many, LANES)).astype(BF)
        ret[:, :feats] = dot(d_pre, gate_full, ((1,), (1,))).astype(BF)
        for e in range(groups):
            ret_to(1, e).start()
        for k in range(1, groups):
            ret_to(0, other(k)).start()
        back[block(mine), :] = ret[block(mine), :]

        hid(far_q, me).wait_recv()
        hid(far_q, pal).start()
        o_down[0] = dot(dx_buf[my_q], hid_buf[my_q], ((0,), (0,)))
        dx_from(far_q).wait_recv()
        o_down[0] += dot(dx_buf[far_q], hid_buf[far_q], ((0,), (0,)))

    @pl.when(end)
    def _():
        for q in (my_q, far_q):
            hid(q, me).wait_recv()
            hid(q, pal).start()
        dx_from(my_q).wait_recv()
        dx_from(far_q).wait_recv()
        o_down[0] = (dot(dx_buf[my_q], hid_buf[my_q], ((0,), (0,)))
                     + dot(dx_buf[far_q], hid_buf[far_q], ((0,), (0,))))

    for q in (pal_q, fpal_q):
        hid(q, me).wait_recv()
        dx_from(q).wait_recv()
        o_down[0] += dot(dx_buf[q], hid_buf[q], ((0,), (0,)))

    for k in range(1, groups):
        back_from(other(k)).wait_recv()
    pl.when(end)(lambda: back_from(mine).wait_recv())
    o_tok[...] = dot(pick, back[:, :feats]).astype(BF)
    weighted = pick_t * back[:, feats:feats + 1].astype(F32)
    o_gates[...] = jnp.concatenate(
        [jnp.sum(jnp.where(hit, weighted, 0.0), axis=0, keepdims=True) for hit in hits],
        axis=0).astype(BF)

    for p in range(3):
        for way in range(2):
            piece(me, p, way, True).wait_send()

    @pl.when(end)
    def _():
        for e in range(groups):
            slots_to(e, 1).wait_send()
        for p in range(3):
            piece(pal, p, 0).wait_send()
        for q in (my_q, far_q):
            hid(q, pal).wait_send()
        for i in (4, 5):
            local[i].wait()

    @pl.when(mid)
    def _():
        for s, p, way in ((a, 0, 0), (a, 1, 0), (a, 2, 0), (c, 0, 0), (c, 2, 0),
                          (d, 1, 1), (e_, 0, 1), (e_, 1, 1), (e_, 2, 1)):
            piece(s, p, way).wait_send()
        for k in range(1, groups):
            slots_to(other(k), 0).wait_send()
            ret_to(0, other(k)).wait_send()
        for e in range(groups):
            ret_to(1, e).wait_send()
        for s in (far_end, far_mid, my_end, pal):
            hid(my_q, s).wait_send()
        hid(far_q, pal).wait_send()
        for s in (a, b, c, d, e_, f, g):
            dx_to(s).wait_send()


def place(*refs):
    ins, outs, sem = refs[:3], refs[3:6], refs[6]
    copies = [pltpu.make_async_copy(src, dst, sem.at[i]) for i, (src, dst) in enumerate(zip(ins, outs))]
    for c in copies:
        c.start()
    for c in copies:
        c.wait()


def place_whole(*refs):
    for src, dst in zip(refs[:3], refs[3:]):
        dst[...] = src[...]


def solution(mesh):
    groups = mesh.shape["expert"]
    n = mesh.shape["dp"]
    inner = 1
    while n % (inner * 2) == 0 and (inner * 2) ** 2 <= n:
        inner *= 2
    outer = n // inner

    def on_device(tokens, d_output, expert_ids, gate_scores, gate_up_w, down_w):
        feats = tokens.shape[1]
        rows = gate_up_w.shape[1]
        width = down_w.shape[2]
        slots = groups * PAD
        packed = groups * CAP
        vmem = pl.BlockSpec(memory_space=pltpu.VMEM)
        dma = pltpu.SemaphoreType.DMA
        grads, d_gates, d_down = pl.pallas_call(
            functools.partial(ring_kernel, groups, outer, inner),
            out_shape=(
                jax.ShapeDtypeStruct(tokens.shape, BF),
                jax.ShapeDtypeStruct(gate_scores.shape[::-1], BF),
                jax.ShapeDtypeStruct(down_w.shape, F32),
            ),
            in_specs=[vmem] * 6,
            out_specs=(vmem,) * 3,
            scratch_shapes=[
                pltpu.VMEM((n, rows, 2 * width), BF),
                pltpu.VMEM((n, rows, width), BF),
                pltpu.VMEM((n, slots, rows), BF),
                pltpu.VMEM((n, slots, rows), BF),
                pltpu.VMEM((slots, 2 * width), F32),
                pltpu.VMEM((slots, width), F32),
                pltpu.VMEM((slots, 2 * feats + LANES), BF),
                pltpu.VMEM((slots, 2 * feats + LANES), BF),
                pltpu.VMEM((n, packed, width), BF),
                pltpu.VMEM((n, packed, rows), BF),
                pltpu.VMEM((n, packed, rows), BF),
                pltpu.VMEM((slots, feats + LANES), BF),
                pltpu.VMEM((slots, feats + LANES), BF),
                dma((2, 4, n)), dma((2, n)), dma((2,)),
                dma((groups,)), dma((groups,)),
                dma((n,)), dma((n,)),
                dma((n,)), dma((n,)),
                dma((groups,)), dma((groups,)),
            ],
            compiler_params=pltpu.CompilerParams(
                collective_id=0, has_side_effects=True, vmem_limit_bytes=60 * 2**20),
        )(tokens, d_output, expert_ids.T, gate_scores.T, gate_up_w, down_w)
        grads, d_gates, d_down = pl.pallas_call(
            place_whole,
            out_shape=tuple(jax.ShapeDtypeStruct(v.shape, v.dtype) for v in (grads, d_gates, d_down)),
            in_specs=[vmem] * 3,
            out_specs=(vmem,) * 3,
        )(grads, d_gates, d_down)
        return grads, d_gates.T, d_down

    def paired(tokens, d_output, expert_ids, gate_scores, gate_up_w, down_w):
        t_rows, feats = tokens.shape
        topk = expert_ids.shape[1]
        rows = gate_up_w.shape[1]
        width = down_w.shape[2]
        slots = groups * PAD
        packed = 2 * groups * CAP
        vmem = pl.BlockSpec(memory_space=pltpu.VMEM)
        hbm = pl.BlockSpec(memory_space=pltpu.HBM)
        dma = pltpu.SemaphoreType.DMA
        shapes = (
            jax.ShapeDtypeStruct(tokens.shape, BF),
            jax.ShapeDtypeStruct(gate_scores.shape[::-1], BF),
            jax.ShapeDtypeStruct(down_w.shape, F32),
        )
        parts = pl.pallas_call(
            functools.partial(mid_kernel, groups),
            out_shape=shapes,
            in_specs=[hbm] * 6,
            out_specs=(vmem,) * 3,
            scratch_shapes=[
                pltpu.VMEM((n, rows, 2 * width), BF),
                pltpu.VMEM((n, rows, width), BF),
                pltpu.VMEM((t_rows, feats), BF),
                pltpu.VMEM((t_rows, feats), BF),
                pltpu.VMEM((topk, t_rows), jnp.int32),
                pltpu.VMEM((topk, t_rows), BF),
                pltpu.VMEM((slots, 2 * feats + LANES), BF),
                pltpu.VMEM((2 * slots, 2 * feats + LANES), BF),
                pltpu.VMEM((2 * slots, 2 * width), F32),
                pltpu.VMEM((2 * slots, width), F32),
                pltpu.VMEM((n, packed, rows), BF),
                pltpu.VMEM((4, packed, rows), BF),
                pltpu.VMEM((4, packed, width), BF),
                pltpu.VMEM((2 * slots, feats + LANES), BF),
                pltpu.VMEM((slots, feats + LANES), BF),
                dma((6,)),
                dma((2, n, 3)), dma((n, 3)),
                dma((groups,)), dma((2, groups)),
                dma((n,)), dma((4,)),
                dma((4, n)), dma((4,)),
                dma((2, groups)), dma((groups,)),
            ],
            compiler_params=pltpu.CompilerParams(
                collective_id=0, has_side_effects=True, vmem_limit_bytes=16 * 2**20),
        )(*(pltpu.with_memory_space_constraint(v, pltpu.HBM) for v in (
            gate_up_w, down_w, tokens, d_output, expert_ids.T, gate_scores.T)))
        grads, d_gates, d_down = pl.pallas_call(
            place,
            out_shape=shapes,
            in_specs=[vmem] * 3,
            out_specs=(hbm,) * 3,
            scratch_shapes=[dma((3,))],
            compiler_params=pltpu.CompilerParams(vmem_limit_bytes=2**20),
        )(*parts)
        return grads, d_gates.T, d_down

    lines = inner == 2 and outer == 4
    tok = P(("expert", "dp"), None)
    w = P("expert", "dp", None)
    return jax.shard_map(
        paired if lines else on_device, mesh=mesh, in_specs=(tok, tok, tok, tok, w, w),
        out_specs=(tok, tok, w), check_vma=False)
```

```python
import functools

import jax
import jax.numpy as jnp
from jax import lax
from jax.experimental import pallas as pl
from jax.experimental.pallas import tpu as pltpu
from jax.sharding import PartitionSpec as P

CAP = 12
PAD = 16
LANES = 128
FOLD = CAP // (PAD - CAP)
BF = jnp.bfloat16
F32 = jnp.float32


def dot(left, right, dims=((1,), (0,))):
    return lax.dot_general(left, right, (dims, ((), ())), preferred_element_type=F32)


def ring_kernel(groups, outer, inner, tok, dout, ids, scores, gate_in, down_in,
           o_tok, o_gates, o_down,
           gate_buf, down_buf, x_ch, up_ch, pre_acc, u_acc, send, recv, hid_buf, dx_send, dx_buf, ret, back,
           w_send, w_recv, own_sem, s_send, s_recv, h_send, h_recv, x_send, x_recv, b_send, b_recv):
    n = outer * inner
    me = lax.axis_index("dp")
    mine = lax.axis_index("expert")
    zo = me // inner
    xi = me - zo * inner
    slots = groups * PAD
    rows = gate_in.shape[1]
    feats = tok.shape[1]
    width = down_in.shape[2]
    ins = (down_in, gate_in)
    bufs = (down_buf, gate_buf)

    barrier = pltpu.get_barrier_semaphore()
    for k in range(1, n):
        pl.semaphore_signal(barrier, inc=1, device_id={"dp": lax.rem(me + k, n)},
                            device_id_type=pl.DeviceIdType.MESH)
    for k in range(1, groups):
        pl.semaphore_signal(barrier, inc=1, device_id={"expert": lax.rem(mine + k, groups)},
                            device_id_type=pl.DeviceIdType.MESH)
    pl.semaphore_wait(barrier, n - 1 + groups - 1)

    def remote(src, dst, ss, rs, **where):
        return pltpu.make_async_remote_copy(
            src_ref=src, dst_ref=dst, send_sem=ss, recv_sem=rs,
            device_id=where, device_id_type=pl.DeviceIdType.MESH)

    def target(way):
        return me + (inner, -inner, 1, -1)[way]

    def can(way):
        return (zo < outer - 1, zo > 0, xi < inner - 1, xi > 0)[way]

    def hop(w, s, way, own=False):
        src = ins[w].at[0] if own else bufs[w].at[s]
        return remote(src, bufs[w].at[s], w_send.at[w, way, s], w_recv.at[w, s], dp=target(way))

    started = []
    accs = (u_acc, pre_acc)
    chunks = (up_ch, x_ch)

    def forward(w, s, way, valid, own=False):
        ok = can(way) if valid is None else jnp.logical_and(can(way), valid)

        @pl.when(ok)
        def _():
            hop(w, s, way, own).start()
        started.append((ok, w, s, way, own))

    def arrive(w, s, valid):
        @pl.when(valid)
        def _():
            hop(w, s, 0).wait_recv()

    def add(w, s, valid):
        @pl.when(valid)
        def _():
            accs[w][...] += dot(chunks[w][s], bufs[w][s])

    def outer_shards(d):
        return ((0, me - d * inner, zo >= d), (1, me + d * inner, zo + d < outer))

    def outer_step(w, d):
        for way, s, valid in outer_shards(d):
            arrive(w, s, valid)
            for go in (way, 2, 3):
                forward(w, s, go, valid)

    def outer_add(w, d):
        for _, s, valid in outer_shards(d):
            add(w, s, valid)

    def inner_step(w, d):
        for di in range(1, inner):
            for sign in ((1,) if d == 0 else (-1, 1)):
                so = zo + sign * d
                good = jnp.logical_and(so >= 0, so < outer)
                for way, step in ((2, -di), (3, di)):
                    xs = xi + step
                    valid = jnp.logical_and(good, jnp.logical_and(xs >= 0, xs < inner))
                    s = so * inner + xs
                    arrive(w, s, valid)
                    if inner > 2:
                        forward(w, s, way, valid)
                    add(w, s, valid)

    own = [pltpu.make_async_copy(ins[w].at[0], bufs[w].at[me], own_sem.at[w]) for w in range(2)]
    for way in range(4):
        forward(1, me, way, None, own=True)
    for way in range(4):
        forward(0, me, way, None, own=True)
    for c in own:
        c.start()

    t_rows = tok.shape[0]
    topk = ids.shape[0]
    row = lax.broadcasted_iota(jnp.int32, (slots, t_rows), 0)
    row_e = row // PAD
    row_r = (row - row_e * PAD).astype(F32)
    idv = ids[...]
    scv = scores[...].astype(F32)
    live = jnp.zeros((slots, t_rows), F32)
    gcol = jnp.zeros((slots, t_rows), F32)
    hits = []
    for k in range(topk):
        hit = idv[k:k + 1, :] == row_e
        hits.append(hit)
        live = jnp.where(hit, 1.0, live)
        gcol = jnp.where(hit, scv[k:k + 1, :], gcol)
    upper = (lax.broadcasted_iota(jnp.int32, (t_rows, t_rows), 0)
             < lax.broadcasted_iota(jnp.int32, (t_rows, t_rows), 1))
    rank = dot(live.astype(BF), jnp.where(upper, 1.0, 0.0).astype(BF))
    pick_t = jnp.where(rank == row_r, live, 0.0)
    pick_b = pick_t.astype(BF)
    send[:, 2 * feats:] = jnp.broadcast_to(
        jnp.sum(pick_t * gcol, axis=1, keepdims=True), (slots, LANES)).astype(BF)
    send[:, :feats] = dot(pick_b, tok[...]).astype(BF)
    send[:, feats:2 * feats] = dot(pick_b, dout[...]).astype(BF)

    def block(e):
        return pl.ds(pl.multiple_of(e * PAD, PAD), PAD)

    def swap(src, dst, ss, rs, k):
        e = lax.rem(mine + k, groups)
        return remote(src.at[block(e), :], dst.at[block(mine), :], ss.at[k], rs.at[k], expert=e)

    for k in range(1, groups):
        swap(send, recv, s_send, s_recv, k).start()
    recv[block(mine), :] = send[block(mine), :]
    pick = jnp.transpose(pick_t).astype(BF)

    def peer(src, dst, ss, rs, k, sliced):
        d = lax.rem(me + k, n)
        return remote(src.at[d] if sliced else src.at[me], dst.at[me], ss.at[k], rs.at[k], dp=d)

    if outer > 1:
        outer_step(1, 1)
        outer_step(0, 1)

    packed = groups * CAP
    pr = lax.broadcasted_iota(jnp.int32, (packed, slots), 0)
    pc = lax.broadcasted_iota(jnp.int32, (packed, slots), 1)
    pack = jnp.where(pc == (pr // CAP) * PAD + pr % CAP, 1.0, 0.0).astype(BF)

    for k in range(1, groups):
        swap(send, recv, s_send, s_recv, k).wait_recv()
    gates = recv[:, 2 * feats:2 * feats + 1].astype(F32)
    upstream = recv[:, feats:2 * feats]
    dexp = dot(pack, (gates * upstream.astype(F32)).astype(BF)).astype(BF)
    for d in range(n):
        dx_send[d] = dexp[:, d * rows:(d + 1) * rows]
        x_ch[d] = recv[:, d * rows:(d + 1) * rows]
        up_ch[d] = recv[:, feats + d * rows:feats + (d + 1) * rows]
    for k in range(1, n):
        peer(dx_send, dx_buf, x_send, x_recv, k, True).start()
    dx_buf[me] = dx_send[me]
    pre_acc[...] = dot(x_ch[me], gate_in[0])
    u_acc[...] = dot(up_ch[me], down_in[0])

    for d in range(2, outer):
        outer_step(1, d)
        outer_step(0, d)
        outer_add(1, d - 1)
        outer_add(0, d - 1)
    for d in range(outer - 1):
        inner_step(1, d)
        inner_step(0, d)
    if outer > 1:
        outer_add(1, outer - 1)
        outer_add(0, outer - 1)
    inner_step(1, outer - 1)

    pre = pre_acc[...]
    a = pre[:, :width]
    b = pre[:, width:]
    sig = jax.nn.sigmoid(a)
    act = a * sig
    hidden = (act * b).astype(BF)
    hid_buf[me] = dot(pack, hidden).astype(BF)
    for k in range(1, n):
        peer(hid_buf, hid_buf, h_send, h_recv, k, False).start()

    inner_step(0, outer - 1)
    for c in own:
        c.wait()

    u = u_acc[...]
    d_hid = gates * u
    d_pre = jnp.concatenate(
        [d_hid * b * sig * (1.0 + a * (1.0 - sig)), d_hid * act], axis=1).astype(BF)
    gate_full = gate_buf[...].reshape(n * rows, 2 * width)
    ret[:, feats:] = jnp.broadcast_to(
        jnp.sum(hidden.astype(F32) * u, axis=1, keepdims=True), (slots, LANES)).astype(BF)
    ret[:, :feats] = dot(d_pre, gate_full, ((1,), (1,))).astype(BF)
    for k in range(1, groups):
        swap(ret, back, b_send, b_recv, k).start()
    back[block(mine), :] = ret[block(mine), :]

    o_down[0] = dot(dx_buf[me], hid_buf[me], ((0,), (0,)))
    for k in range(1, n):
        s = lax.rem(me - k + n, n)
        peer(dx_send, dx_buf, x_send, x_recv, k, True).wait_recv()
        peer(hid_buf, hid_buf, h_send, h_recv, k, False).wait_recv()
        o_down[0] += dot(dx_buf[s], hid_buf[s], ((0,), (0,)))

    for k in range(1, groups):
        swap(ret, back, b_send, b_recv, k).wait_recv()
    o_tok[...] = dot(pick, back[:, :feats]).astype(BF)
    weighted = pick_t * back[:, feats:feats + 1].astype(F32)
    o_gates[...] = jnp.concatenate(
        [jnp.sum(jnp.where(hit, weighted, 0.0), axis=0, keepdims=True) for hit in hits],
        axis=0).astype(BF)

    for ok, w, s, way, is_own in started:
        @pl.when(ok)
        def _(w=w, s=s, way=way, is_own=is_own):
            hop(w, s, way, is_own).wait_send()
    for k in range(1, groups):
        swap(send, recv, s_send, s_recv, k).wait_send()
        swap(ret, back, b_send, b_recv, k).wait_send()
    for k in range(1, n):
        peer(dx_send, dx_buf, x_send, x_recv, k, True).wait_send()
        peer(hid_buf, hid_buf, h_send, h_recv, k, False).wait_send()

def remote(src, dst, ss, rs, **where):
    return pltpu.make_async_remote_copy(
        src_ref=src, dst_ref=dst, send_sem=ss, recv_sem=rs,
        device_id=where, device_id_type=pl.DeviceIdType.MESH)


def spread(blocks, j, down):
    size = blocks * PAD
    r = lax.broadcasted_iota(jnp.int32, (size, size), 0)
    c = lax.broadcasted_iota(jnp.int32, (size, size), 1)
    if not down:
        r, c = c, r
    i = r % PAD - CAP
    hit = jnp.logical_and(jnp.logical_and(r // PAD == c // PAD, i >= 0), c % PAD == FOLD * i + j)
    return jnp.where(hit, 1.0, 0.0).astype(BF)


def mid_kernel(groups, gate_in, down_in, tok_in, dout_in, ids_in, sc_in,
               o_tok, o_gates, o_down,
               gate_buf, down_buf, tok_v, dout_v, ids_v, sc_v, x_out, d_out, x_in, d_in, pre_acc, v_acc,
               dx_send, dx_buf, hid_buf, ret_a, ret_b, back_a, back_b,
               l_sem, w_send, w_recv, s_send, s_recv, x_send, x_recv,
               h_send, h_recv, b_send, b_recv):
    me = lax.axis_index("dp")
    mine = lax.axis_index("expert")
    zo = me // 2
    xi = me - 2 * zo
    side = zo // 2
    mid = jnp.logical_or(zo == 1, zo == 2)
    end = jnp.logical_not(mid)
    slots = groups * PAD
    rows = gate_in.shape[1]
    feats = tok_in.shape[1]
    width = down_in.shape[2]
    n = feats // rows

    def at(x, z):
        return 2 * z + x

    xo = 1 - xi
    pal = at(xo, zo)
    z_mid, z_end, z_far, z_edge = 1 + side, 3 * side, 2 - side, 3 - 3 * side
    my_mid, my_end = at(xi, z_mid), at(xi, z_end)
    far_mid, far_end = at(xi, z_far), at(xi, z_edge)
    line = jnp.where(mid, far_mid, my_mid)

    barrier = pltpu.get_barrier_semaphore()

    def greet(**where):
        pl.semaphore_signal(barrier, inc=1, device_id=where, device_id_type=pl.DeviceIdType.MESH)

    greet(dp=pal)

    @pl.when(mid)
    def _():
        greet(dp=far_mid)
        for e in range(groups):
            greet(dp=my_end, expert=e)
        for k in range(1, groups):
            greet(expert=lax.rem(mine + k, groups))

    local = [pltpu.make_async_copy(src, dst, l_sem.at[i]) for i, (src, dst) in enumerate((
        (ids_in, ids_v), (sc_in, sc_v), (tok_in, tok_v), (dout_in, dout_v),
        (gate_in.at[0], gate_buf.at[me]), (down_in.at[0], down_buf.at[me])))]
    for c in local:
        c.start()
    pl.semaphore_wait(barrier, 1 + groups)

    def piece(s, p, way, own=False):
        if p < 4:
            part = pl.ds(p * (rows // 4), rows // 4)
            src = gate_in.at[0, part] if own else gate_buf.at[s, part]
            dst = gate_buf.at[s, part]
        else:
            part = pl.ds((p - 4) * (rows // 2), rows // 2)
            src = down_in.at[0, part] if own else down_buf.at[s, part]
            dst = down_buf.at[s, part]
        return remote(src, dst, w_send.at[way, s, p], w_recv.at[s, p], dp=(line, pal)[way])

    def own_out(way, *ps):
        for p in ps:
            piece(me, p, way, True).start()

    def take(s, p, *out):
        piece(s, p, 0).wait_recv()
        for way in out:
            piece(s, p, way).start()

    for p in range(4):
        own_out(0, p)
        own_out(1, p)

    @pl.when(end)
    def _():
        for p in (4, 5):
            own_out(0, p)
            own_out(1, p)

    for c in local[:4]:
        c.wait()
    t_rows = tok_v.shape[0]
    topk = ids_v.shape[0]
    row = lax.broadcasted_iota(jnp.int32, (slots, t_rows), 0)
    row_e = row // PAD
    row_r = (row - row_e * PAD).astype(F32)
    idv = ids_v[...]
    scv = sc_v[...].astype(F32)
    live = jnp.zeros((slots, t_rows), F32)
    gcol = jnp.zeros((slots, t_rows), F32)
    hits = []
    for k in range(topk):
        hit = idv[k:k + 1, :] == row_e
        hits.append(hit)
        live = jnp.where(hit, 1.0, live)
        gcol = jnp.where(hit, scv[k:k + 1, :], gcol)
    upper = (lax.broadcasted_iota(jnp.int32, (t_rows, t_rows), 0)
             < lax.broadcasted_iota(jnp.int32, (t_rows, t_rows), 1))
    rank = dot(live.astype(BF), jnp.where(upper, 1.0, 0.0).astype(BF))
    pick_t = jnp.where(rank == row_r, live, 0.0)
    pick_b = pick_t.astype(BF)
    gate_col = jnp.sum(pick_t * gcol, axis=1, keepdims=True)

    def block(i):
        start = i * PAD
        return pl.ds(start if isinstance(i, int) else pl.multiple_of(start, PAD), PAD)

    outs, ins = (x_out, d_out), (x_in, d_in)

    def slots_to(kind, e, place):
        return remote(outs[kind].at[block(e), :], ins[kind].at[block(place * groups + mine), :],
                      s_send.at[kind, e], s_recv.at[kind, place, mine], dp=my_mid, expert=e)

    def slots_from(kind, place, e):
        return remote(outs[kind].at[block(e), :], ins[kind].at[block(place * groups + e), :],
                      s_send.at[kind, e], s_recv.at[kind, place, e], dp=my_mid, expert=e)

    def other(k):
        return lax.rem(mine + k, groups)

    def slots_out(kind):
        @pl.when(end)
        def _():
            for e in range(groups):
                slots_to(kind, e, 1).start()

        @pl.when(mid)
        def _():
            for k in range(1, groups):
                slots_to(kind, other(k), 0).start()
            ins[kind][block(mine), :] = outs[kind][block(mine), :]

    x_out[...] = dot(pick_b, tok_v[...]).astype(BF)
    slots_out(0)
    d_out[:, feats:] = jnp.broadcast_to(gate_col, (slots, LANES)).astype(BF)
    d_out[:, :feats] = (gate_col * dot(pick_b, dout_v[...])).astype(BF)

    @pl.when(end)
    def _():
        for p in range(4):
            take(pal, p, 0)

    slots_out(1)

    @pl.when(end)
    def _():
        for p in (4, 5):
            take(pal, p, 0)

    pick = jnp.transpose(pick_t).astype(BF)
    folded = [dot(pick, spread(groups, j, False)).astype(BF) for j in range(FOLD)]

    def dx_to(d):
        return remote(dx_send.at[d], dx_buf.at[2 * side + xi], x_send.at[d], x_recv.at[2 * side + xi], dp=d)

    def dx_from(q):
        return remote(dx_send.at[0], dx_buf.at[q], x_send.at[0], x_recv.at[q], dp=pal)

    def hid(q, d):
        return remote(hid_buf.at[q], hid_buf.at[q], h_send.at[q, d], h_recv.at[q], dp=d)

    rets, backs = (ret_a, ret_b), (back_a, back_b)

    def ret_to(part, place, e):
        return remote(rets[part].at[block(place * groups + e), :], backs[part].at[block(mine), :],
                      b_send.at[part, place, e], b_recv.at[part, mine], dp=(my_mid, my_end)[place], expert=e)

    def back_from(part, e):
        return remote(rets[part].at[block(e), :], backs[part].at[block(e), :],
                      b_send.at[part, 0, e], b_recv.at[part, e], dp=my_mid, expert=e)

    def ret_out(part):
        for e in range(groups):
            ret_to(part, 1, e).start()
        for k in range(1, groups):
            ret_to(part, 0, other(k)).start()
        backs[part][block(mine), :] = rets[part][block(mine), :]

    my_q, pal_q = 2 * side + xi, 2 * side + xo
    far_q, fpal_q = 2 - 2 * side + xi, 2 - 2 * side + xo
    a, b, c, d, e_, f, g = (my_end, at(xo, z_end), pal, far_mid, far_end, at(xo, z_far), at(xo, z_edge))

    @pl.when(mid)
    def _():
        many = 2 * slots
        packed = 2 * groups * CAP

        def cols(s):
            return pl.ds(pl.multiple_of(s * rows, LANES), rows)

        def add(s):
            pre_acc[...] += dot(x_in[:, cols(s)], gate_buf[s])

        def add_v(s):
            v_acc[...] += dot(d_in[:, cols(s)], down_buf[s])

        def slots_wait(kind):
            for k in range(1, groups):
                slots_from(kind, 0, other(k)).wait_recv()
            for e in range(groups):
                slots_from(kind, 1, e).wait_recv()

        take(a, 0, 0)
        take(a, 1, 0)
        take(d, 2, 1)
        take(a, 2, 0)
        take(d, 3, 1)
        take(a, 3, 0)
        take(c, 0, 0)
        take(c, 1, 0)
        own_out(0, 4, 5)
        take(a, 4, 0)
        take(a, 5, 0)
        for p in range(4):
            take(e_, p, 1)
        own_out(1, 4, 5)
        slots_wait(0)
        local[4].wait()
        pre_acc[...] = dot(x_in[:, cols(me)], gate_buf[me])
        take(c, 2)
        take(c, 3)
        take(d, 0)
        take(d, 1)
        for s in (a, c, d, e_):
            add(s)
        for s in (f, g, b):
            for p in range(4):
                take(s, p)
            add(s)

        pr = lax.broadcasted_iota(jnp.int32, (packed, many), 0)
        pc = lax.broadcasted_iota(jnp.int32, (packed, many), 1)
        pack = jnp.where(pc == (pr // CAP) * PAD + pr % CAP, 1.0, 0.0).astype(BF)
        pre = pre_acc[...]
        ga = pre[:, :width]
        gb = pre[:, width:]
        sig = jax.nn.sigmoid(ga)
        act = ga * sig
        slope = gb * sig * (1.0 + ga * (1.0 - sig))
        hidden = (act * gb).astype(BF)
        hid_buf[my_q] = dot(pack, hidden).astype(BF)
        hid(my_q, my_end).start()
        take(c, 4, 0)
        take(d, 5, 1)
        take(e_, 4, 1)
        take(e_, 5, 1)
        for s in (far_end, pal, far_mid):
            hid(my_q, s).start()

        slots_wait(1)
        local[5].wait()
        dexp = dot(pack, d_in[:, :feats]).astype(BF)
        for s in range(n):
            dx_send[s] = dexp[:, s * rows:(s + 1) * rows]
        for s in (e_, g, a, b, d, f, c):
            dx_to(s).start()
        dx_buf[my_q] = dx_send[me]
        gates = d_in[:, feats:feats + 1].astype(F32)
        inverse = jnp.where(gates > 0.0, 1.0 / jnp.where(gates > 0.0, gates, 1.0), 0.0)
        v_acc[...] = dot(d_in[:, cols(me)], down_buf[me])
        take(c, 5)
        take(d, 4)
        for s in (a, c, d, e_):
            add_v(s)
        for s in (f, b, g):
            take(s, 4)
            take(s, 5)
            add_v(s)

        d_hid = v_acc[...]
        d_pre = jnp.concatenate([d_hid * slope, d_hid * act], axis=1).astype(BF)
        quarter = feats // 4

        def d_slot(j):
            w = gate_buf[j * n // 4:(j + 1) * n // 4].reshape(quarter, 2 * width)
            return dot(d_pre, w, ((1,), (1,)))

        last = d_slot(3).astype(BF)

        def fold(j):
            return (d_slot(j) + dot(spread(2 * groups, j, True), last)).astype(BF)

        ret_a[...] = fold(0)
        ret_out(0)
        for j in range(1, FOLD):
            ret_b[:, (j - 1) * quarter:j * quarter] = fold(j)
        slot_grad = jnp.sum(hidden.astype(F32) * d_hid, axis=1, keepdims=True) * inverse
        ret_b[:, 2 * quarter:] = jnp.broadcast_to(slot_grad, (many, LANES)).astype(BF)
        ret_out(1)

        hid(far_q, me).wait_recv()
        hid(far_q, pal).start()
        o_down[0] = dot(dx_buf[my_q], hid_buf[my_q], ((0,), (0,)))
        dx_from(far_q).wait_recv()
        o_down[0] += dot(dx_buf[far_q], hid_buf[far_q], ((0,), (0,)))

    @pl.when(end)
    def _():
        for q in (my_q, far_q):
            hid(q, me).wait_recv()
            hid(q, pal).start()
        dx_from(my_q).wait_recv()
        dx_from(far_q).wait_recv()
        o_down[0] = (dot(dx_buf[my_q], hid_buf[my_q], ((0,), (0,)))
                     + dot(dx_buf[far_q], hid_buf[far_q], ((0,), (0,))))

    def grow(q):
        hid(q, me).wait_recv()
        dx_from(q).wait_recv()
        o_down[0] += dot(dx_buf[q], hid_buf[q], ((0,), (0,)))

    grow(pal_q)
    quarter = feats // 4

    def back_wait(part):
        for k in range(1, groups):
            back_from(part, other(k)).wait_recv()
        pl.when(end)(lambda: back_from(part, mine).wait_recv())

    back_wait(0)
    o_tok[:, :quarter] = dot(pick, back_a[...]).astype(BF)
    last = dot(folded[0], back_a[...])
    back_wait(1)
    for j in range(1, FOLD):
        part = back_b[:, (j - 1) * quarter:j * quarter]
        o_tok[:, j * quarter:(j + 1) * quarter] = dot(pick, part).astype(BF)
        last += dot(folded[j], part)
    o_tok[:, 3 * quarter:] = last.astype(BF)
    weighted = pick_t * back_b[:, 2 * quarter:2 * quarter + 1].astype(F32)
    o_gates[...] = jnp.concatenate(
        [jnp.sum(jnp.where(hit, weighted, 0.0), axis=0, keepdims=True) for hit in hits],
        axis=0).astype(BF)
    grow(fpal_q)

    for p in range(6):
        for way in range(2):
            piece(me, p, way, True).wait_send()

    @pl.when(end)
    def _():
        for e in range(groups):
            slots_to(0, e, 1).wait_send()
            slots_to(1, e, 1).wait_send()
        for p in range(6):
            piece(pal, p, 0).wait_send()
        for q in (my_q, far_q):
            hid(q, pal).wait_send()
        for i in (4, 5):
            local[i].wait()

    @pl.when(mid)
    def _():
        for p in range(6):
            piece(a, p, 0).wait_send()
        for s, p, way in ((c, 0, 0), (c, 1, 0), (c, 4, 0), (d, 2, 1), (d, 3, 1), (d, 5, 1)):
            piece(s, p, way).wait_send()
        for p in range(6):
            piece(e_, p, 1).wait_send()
        for k in range(1, groups):
            slots_to(0, other(k), 0).wait_send()
            slots_to(1, other(k), 0).wait_send()
            for part in range(2):
                ret_to(part, 0, other(k)).wait_send()
        for e in range(groups):
            for part in range(2):
                ret_to(part, 1, e).wait_send()
        for s in (far_end, far_mid, my_end, pal):
            hid(my_q, s).wait_send()
        hid(far_q, pal).wait_send()
        for s in (a, b, c, d, e_, f, g):
            dx_to(s).wait_send()


def place(*refs):
    ins, outs, sem = refs[:3], refs[3:6], refs[6]
    copies = [pltpu.make_async_copy(src, dst, sem.at[i]) for i, (src, dst) in enumerate(zip(ins, outs))]
    for c in copies:
        c.start()
    for c in copies:
        c.wait()


def place_whole(*refs):
    for src, dst in zip(refs[:3], refs[3:]):
        dst[...] = src[...]


def solution(mesh):
    groups = mesh.shape["expert"]
    n = mesh.shape["dp"]
    inner = 1
    while n % (inner * 2) == 0 and (inner * 2) ** 2 <= n:
        inner *= 2
    outer = n // inner

    def on_device(tokens, d_output, expert_ids, gate_scores, gate_up_w, down_w):
        feats = tokens.shape[1]
        rows = gate_up_w.shape[1]
        width = down_w.shape[2]
        slots = groups * PAD
        packed = groups * CAP
        vmem = pl.BlockSpec(memory_space=pltpu.VMEM)
        dma = pltpu.SemaphoreType.DMA
        grads, d_gates, d_down = pl.pallas_call(
            functools.partial(ring_kernel, groups, outer, inner),
            out_shape=(
                jax.ShapeDtypeStruct(tokens.shape, BF),
                jax.ShapeDtypeStruct(gate_scores.shape[::-1], BF),
                jax.ShapeDtypeStruct(down_w.shape, F32),
            ),
            in_specs=[vmem] * 6,
            out_specs=(vmem,) * 3,
            scratch_shapes=[
                pltpu.VMEM((n, rows, 2 * width), BF),
                pltpu.VMEM((n, rows, width), BF),
                pltpu.VMEM((n, slots, rows), BF),
                pltpu.VMEM((n, slots, rows), BF),
                pltpu.VMEM((slots, 2 * width), F32),
                pltpu.VMEM((slots, width), F32),
                pltpu.VMEM((slots, 2 * feats + LANES), BF),
                pltpu.VMEM((slots, 2 * feats + LANES), BF),
                pltpu.VMEM((n, packed, width), BF),
                pltpu.VMEM((n, packed, rows), BF),
                pltpu.VMEM((n, packed, rows), BF),
                pltpu.VMEM((slots, feats + LANES), BF),
                pltpu.VMEM((slots, feats + LANES), BF),
                dma((2, 4, n)), dma((2, n)), dma((2,)),
                dma((groups,)), dma((groups,)),
                dma((n,)), dma((n,)),
                dma((n,)), dma((n,)),
                dma((groups,)), dma((groups,)),
            ],
            compiler_params=pltpu.CompilerParams(
                collective_id=0, has_side_effects=True, vmem_limit_bytes=60 * 2**20),
        )(tokens, d_output, expert_ids.T, gate_scores.T, gate_up_w, down_w)
        grads, d_gates, d_down = pl.pallas_call(
            place_whole,
            out_shape=tuple(jax.ShapeDtypeStruct(v.shape, v.dtype) for v in (grads, d_gates, d_down)),
            in_specs=[vmem] * 3,
            out_specs=(vmem,) * 3,
        )(grads, d_gates, d_down)
        return grads, d_gates.T, d_down

    def paired(tokens, d_output, expert_ids, gate_scores, gate_up_w, down_w):
        t_rows, feats = tokens.shape
        topk = expert_ids.shape[1]
        rows = gate_up_w.shape[1]
        width = down_w.shape[2]
        slots = groups * PAD
        packed = 2 * groups * CAP
        vmem = pl.BlockSpec(memory_space=pltpu.VMEM)
        hbm = pl.BlockSpec(memory_space=pltpu.HBM)
        dma = pltpu.SemaphoreType.DMA
        shapes = (
            jax.ShapeDtypeStruct(tokens.shape, BF),
            jax.ShapeDtypeStruct(gate_scores.shape[::-1], BF),
            jax.ShapeDtypeStruct(down_w.shape, F32),
        )
        parts = pl.pallas_call(
            functools.partial(mid_kernel, groups),
            out_shape=shapes,
            in_specs=[hbm] * 6,
            out_specs=(vmem,) * 3,
            scratch_shapes=[
                pltpu.VMEM((n, rows, 2 * width), BF),
                pltpu.VMEM((n, rows, width), BF),
                pltpu.VMEM((t_rows, feats), BF),
                pltpu.VMEM((t_rows, feats), BF),
                pltpu.VMEM((topk, t_rows), jnp.int32),
                pltpu.VMEM((topk, t_rows), BF),
                pltpu.VMEM((slots, feats), BF),
                pltpu.VMEM((slots, feats + LANES), BF),
                pltpu.VMEM((2 * slots, feats), BF),
                pltpu.VMEM((2 * slots, feats + LANES), BF),
                pltpu.VMEM((2 * slots, 2 * width), F32),
                pltpu.VMEM((2 * slots, width), F32),
                pltpu.VMEM((n, packed, rows), BF),
                pltpu.VMEM((4, packed, rows), BF),
                pltpu.VMEM((4, packed, width), BF),
                pltpu.VMEM((2 * slots, feats // 4), BF),
                pltpu.VMEM((2 * slots, feats // 2 + LANES), BF),
                pltpu.VMEM((slots, feats // 4), BF),
                pltpu.VMEM((slots, feats // 2 + LANES), BF),
                dma((6,)),
                dma((2, n, 6)), dma((n, 6)),
                dma((2, groups)), dma((2, 2, groups)),
                dma((n,)), dma((4,)),
                dma((4, n)), dma((4,)),
                dma((2, 2, groups)), dma((2, groups)),
            ],
            compiler_params=pltpu.CompilerParams(
                collective_id=0, has_side_effects=True, vmem_limit_bytes=16 * 2**20),
        )(*(pltpu.with_memory_space_constraint(v, pltpu.HBM) for v in (
            gate_up_w, down_w, tokens, d_output, expert_ids.T, gate_scores.T)))
        grads, d_gates, d_down = pl.pallas_call(
            place,
            out_shape=shapes,
            in_specs=[vmem] * 3,
            out_specs=(hbm,) * 3,
            scratch_shapes=[dma((3,))],
            compiler_params=pltpu.CompilerParams(vmem_limit_bytes=2**20),
        )(*parts)
        return grads, d_gates.T, d_down

    lines = inner == 2 and outer == 4
    tok = P(("expert", "dp"), None)
    w = P("expert", "dp", None)
    return jax.shard_map(
        paired if lines else on_device, mesh=mesh, in_specs=(tok, tok, tok, tok, w, w),
        out_specs=(tok, tok, w), check_vma=False)
```

```python
import functools

import jax
import jax.numpy as jnp
from jax import lax
from jax.experimental import pallas as pl
from jax.experimental.pallas import tpu as pltpu
from jax.sharding import PartitionSpec as P

CAP = 12
PAD = 16
LANES = 128
FOLD = CAP // (PAD - CAP)
BF = jnp.bfloat16
F32 = jnp.float32


def dot(left, right, dims=((1,), (0,))):
    return lax.dot_general(left, right, (dims, ((), ())), preferred_element_type=F32)


def ring_kernel(groups, outer, inner, tok, dout, ids, scores, gate_in, down_in,
           o_tok, o_gates, o_down,
           gate_buf, down_buf, x_ch, up_ch, pre_acc, u_acc, send, recv, hid_buf, dx_send, dx_buf, ret, back,
           w_send, w_recv, own_sem, s_send, s_recv, h_send, h_recv, x_send, x_recv, b_send, b_recv):
    n = outer * inner
    me = lax.axis_index("dp")
    mine = lax.axis_index("expert")
    zo = me // inner
    xi = me - zo * inner
    slots = groups * PAD
    rows = gate_in.shape[1]
    feats = tok.shape[1]
    width = down_in.shape[2]
    ins = (down_in, gate_in)
    bufs = (down_buf, gate_buf)

    barrier = pltpu.get_barrier_semaphore()
    for k in range(1, n):
        pl.semaphore_signal(barrier, inc=1, device_id={"dp": lax.rem(me + k, n)},
                            device_id_type=pl.DeviceIdType.MESH)
    for k in range(1, groups):
        pl.semaphore_signal(barrier, inc=1, device_id={"expert": lax.rem(mine + k, groups)},
                            device_id_type=pl.DeviceIdType.MESH)
    pl.semaphore_wait(barrier, n - 1 + groups - 1)

    def remote(src, dst, ss, rs, **where):
        return pltpu.make_async_remote_copy(
            src_ref=src, dst_ref=dst, send_sem=ss, recv_sem=rs,
            device_id=where, device_id_type=pl.DeviceIdType.MESH)

    def target(way):
        return me + (inner, -inner, 1, -1)[way]

    def can(way):
        return (zo < outer - 1, zo > 0, xi < inner - 1, xi > 0)[way]

    def hop(w, s, way, own=False):
        src = ins[w].at[0] if own else bufs[w].at[s]
        return remote(src, bufs[w].at[s], w_send.at[w, way, s], w_recv.at[w, s], dp=target(way))

    started = []
    accs = (u_acc, pre_acc)
    chunks = (up_ch, x_ch)

    def forward(w, s, way, valid, own=False):
        ok = can(way) if valid is None else jnp.logical_and(can(way), valid)

        @pl.when(ok)
        def _():
            hop(w, s, way, own).start()
        started.append((ok, w, s, way, own))

    def arrive(w, s, valid):
        @pl.when(valid)
        def _():
            hop(w, s, 0).wait_recv()

    def add(w, s, valid):
        @pl.when(valid)
        def _():
            accs[w][...] += dot(chunks[w][s], bufs[w][s])

    def outer_shards(d):
        return ((0, me - d * inner, zo >= d), (1, me + d * inner, zo + d < outer))

    def outer_step(w, d):
        for way, s, valid in outer_shards(d):
            arrive(w, s, valid)
            for go in (way, 2, 3):
                forward(w, s, go, valid)

    def outer_add(w, d):
        for _, s, valid in outer_shards(d):
            add(w, s, valid)

    def inner_step(w, d):
        for di in range(1, inner):
            for sign in ((1,) if d == 0 else (-1, 1)):
                so = zo + sign * d
                good = jnp.logical_and(so >= 0, so < outer)
                for way, step in ((2, -di), (3, di)):
                    xs = xi + step
                    valid = jnp.logical_and(good, jnp.logical_and(xs >= 0, xs < inner))
                    s = so * inner + xs
                    arrive(w, s, valid)
                    if inner > 2:
                        forward(w, s, way, valid)
                    add(w, s, valid)

    own = [pltpu.make_async_copy(ins[w].at[0], bufs[w].at[me], own_sem.at[w]) for w in range(2)]
    for way in range(4):
        forward(1, me, way, None, own=True)
    for way in range(4):
        forward(0, me, way, None, own=True)
    for c in own:
        c.start()

    t_rows = tok.shape[0]
    topk = ids.shape[0]
    row = lax.broadcasted_iota(jnp.int32, (slots, t_rows), 0)
    row_e = row // PAD
    row_r = (row - row_e * PAD).astype(F32)
    idv = ids[...]
    scv = scores[...].astype(F32)
    live = jnp.zeros((slots, t_rows), F32)
    gcol = jnp.zeros((slots, t_rows), F32)
    hits = []
    for k in range(topk):
        hit = idv[k:k + 1, :] == row_e
        hits.append(hit)
        live = jnp.where(hit, 1.0, live)
        gcol = jnp.where(hit, scv[k:k + 1, :], gcol)
    upper = (lax.broadcasted_iota(jnp.int32, (t_rows, t_rows), 0)
             < lax.broadcasted_iota(jnp.int32, (t_rows, t_rows), 1))
    rank = dot(live.astype(BF), jnp.where(upper, 1.0, 0.0).astype(BF))
    pick_t = jnp.where(rank == row_r, live, 0.0)
    pick_b = pick_t.astype(BF)
    send[:, 2 * feats:] = jnp.broadcast_to(
        jnp.sum(pick_t * gcol, axis=1, keepdims=True), (slots, LANES)).astype(BF)
    send[:, :feats] = dot(pick_b, tok[...]).astype(BF)
    send[:, feats:2 * feats] = dot(pick_b, dout[...]).astype(BF)

    def block(e):
        return pl.ds(pl.multiple_of(e * PAD, PAD), PAD)

    def swap(src, dst, ss, rs, k):
        e = lax.rem(mine + k, groups)
        return remote(src.at[block(e), :], dst.at[block(mine), :], ss.at[k], rs.at[k], expert=e)

    for k in range(1, groups):
        swap(send, recv, s_send, s_recv, k).start()
    recv[block(mine), :] = send[block(mine), :]
    pick = jnp.transpose(pick_t).astype(BF)

    def peer(src, dst, ss, rs, k, sliced):
        d = lax.rem(me + k, n)
        return remote(src.at[d] if sliced else src.at[me], dst.at[me], ss.at[k], rs.at[k], dp=d)

    if outer > 1:
        outer_step(1, 1)
        outer_step(0, 1)

    packed = groups * CAP
    pr = lax.broadcasted_iota(jnp.int32, (packed, slots), 0)
    pc = lax.broadcasted_iota(jnp.int32, (packed, slots), 1)
    pack = jnp.where(pc == (pr // CAP) * PAD + pr % CAP, 1.0, 0.0).astype(BF)

    for k in range(1, groups):
        swap(send, recv, s_send, s_recv, k).wait_recv()
    gates = recv[:, 2 * feats:2 * feats + 1].astype(F32)
    upstream = recv[:, feats:2 * feats]
    dexp = dot(pack, (gates * upstream.astype(F32)).astype(BF)).astype(BF)
    for d in range(n):
        dx_send[d] = dexp[:, d * rows:(d + 1) * rows]
        x_ch[d] = recv[:, d * rows:(d + 1) * rows]
        up_ch[d] = recv[:, feats + d * rows:feats + (d + 1) * rows]
    for k in range(1, n):
        peer(dx_send, dx_buf, x_send, x_recv, k, True).start()
    dx_buf[me] = dx_send[me]
    pre_acc[...] = dot(x_ch[me], gate_in[0])
    u_acc[...] = dot(up_ch[me], down_in[0])

    for d in range(2, outer):
        outer_step(1, d)
        outer_step(0, d)
        outer_add(1, d - 1)
        outer_add(0, d - 1)
    for d in range(outer - 1):
        inner_step(1, d)
        inner_step(0, d)
    if outer > 1:
        outer_add(1, outer - 1)
        outer_add(0, outer - 1)
    inner_step(1, outer - 1)

    pre = pre_acc[...]
    a = pre[:, :width]
    b = pre[:, width:]
    sig = jax.nn.sigmoid(a)
    act = a * sig
    hidden = (act * b).astype(BF)
    hid_buf[me] = dot(pack, hidden).astype(BF)
    for k in range(1, n):
        peer(hid_buf, hid_buf, h_send, h_recv, k, False).start()

    inner_step(0, outer - 1)
    for c in own:
        c.wait()

    u = u_acc[...]
    d_hid = gates * u
    d_pre = jnp.concatenate(
        [d_hid * b * sig * (1.0 + a * (1.0 - sig)), d_hid * act], axis=1).astype(BF)
    gate_full = gate_buf[...].reshape(n * rows, 2 * width)
    ret[:, feats:] = jnp.broadcast_to(
        jnp.sum(hidden.astype(F32) * u, axis=1, keepdims=True), (slots, LANES)).astype(BF)
    ret[:, :feats] = dot(d_pre, gate_full, ((1,), (1,))).astype(BF)
    for k in range(1, groups):
        swap(ret, back, b_send, b_recv, k).start()
    back[block(mine), :] = ret[block(mine), :]

    o_down[0] = dot(dx_buf[me], hid_buf[me], ((0,), (0,)))
    for k in range(1, n):
        s = lax.rem(me - k + n, n)
        peer(dx_send, dx_buf, x_send, x_recv, k, True).wait_recv()
        peer(hid_buf, hid_buf, h_send, h_recv, k, False).wait_recv()
        o_down[0] += dot(dx_buf[s], hid_buf[s], ((0,), (0,)))

    for k in range(1, groups):
        swap(ret, back, b_send, b_recv, k).wait_recv()
    o_tok[...] = dot(pick, back[:, :feats]).astype(BF)
    weighted = pick_t * back[:, feats:feats + 1].astype(F32)
    o_gates[...] = jnp.concatenate(
        [jnp.sum(jnp.where(hit, weighted, 0.0), axis=0, keepdims=True) for hit in hits],
        axis=0).astype(BF)

    for ok, w, s, way, is_own in started:
        @pl.when(ok)
        def _(w=w, s=s, way=way, is_own=is_own):
            hop(w, s, way, is_own).wait_send()
    for k in range(1, groups):
        swap(send, recv, s_send, s_recv, k).wait_send()
        swap(ret, back, b_send, b_recv, k).wait_send()
    for k in range(1, n):
        peer(dx_send, dx_buf, x_send, x_recv, k, True).wait_send()
        peer(hid_buf, hid_buf, h_send, h_recv, k, False).wait_send()

def remote(src, dst, ss, rs, **where):
    return pltpu.make_async_remote_copy(
        src_ref=src, dst_ref=dst, send_sem=ss, recv_sem=rs,
        device_id=where, device_id_type=pl.DeviceIdType.MESH)


def spread(blocks, j, down):
    size = blocks * PAD
    r = lax.broadcasted_iota(jnp.int32, (size, size), 0)
    c = lax.broadcasted_iota(jnp.int32, (size, size), 1)
    if not down:
        r, c = c, r
    i = r % PAD - CAP
    hit = jnp.logical_and(jnp.logical_and(r // PAD == c // PAD, i >= 0), c % PAD == FOLD * i + j)
    return jnp.where(hit, 1.0, 0.0).astype(BF)


def mid_kernel(groups, gate_in, down_in, tok_in, dout_in, ids_in, sc_in,
               o_tok, o_gates, o_down,
               gate_buf, down_buf, tok_v, dout_v, ids_v, sc_v, x_out, d_out, x_in, d_in, pre_acc, v_acc,
               dx_send, dx_buf, hid_buf, ret_a, ret_b, back_a, back_b,
               l_sem, w_send, w_recv, s_send, s_recv, x_send, x_recv,
               h_send, h_recv, b_send, b_recv):
    me = lax.axis_index("dp")
    mine = lax.axis_index("expert")
    zo = me // 2
    xi = me - 2 * zo
    side = zo // 2
    mid = jnp.logical_or(zo == 1, zo == 2)
    end = jnp.logical_not(mid)
    slots = groups * PAD
    rows = gate_in.shape[1]
    feats = tok_in.shape[1]
    width = down_in.shape[2]
    n = feats // rows

    def at(x, z):
        return 2 * z + x

    xo = 1 - xi
    pal = at(xo, zo)
    z_mid, z_end, z_far, z_edge = 1 + side, 3 * side, 2 - side, 3 - 3 * side
    my_mid, my_end = at(xi, z_mid), at(xi, z_end)
    far_mid, far_end = at(xi, z_far), at(xi, z_edge)
    line = jnp.where(mid, far_mid, my_mid)

    barrier = pltpu.get_barrier_semaphore()

    def greet(**where):
        pl.semaphore_signal(barrier, inc=1, device_id=where, device_id_type=pl.DeviceIdType.MESH)

    greet(dp=pal)

    @pl.when(mid)
    def _():
        greet(dp=far_mid)
        for e in range(groups):
            greet(dp=my_end, expert=e)
        for k in range(1, groups):
            greet(expert=lax.rem(mine + k, groups))

    local = [pltpu.make_async_copy(src, dst, l_sem.at[i]) for i, (src, dst) in enumerate((
        (gate_in.at[0], gate_buf.at[me]), (down_in.at[0], down_buf.at[me]),
        (ids_in, ids_v), (sc_in, sc_v), (tok_in, tok_v), (dout_in, dout_v)))]
    for c in local:
        c.start()
    pl.semaphore_wait(barrier, 1 + groups)

    def piece(s, p, way, own=False):
        if p < 4:
            part = pl.ds(p * (rows // 4), rows // 4)
            src = gate_buf.at[s, part]
            dst = gate_buf.at[s, part]
        else:
            part = pl.ds((p - 4) * (rows // 2), rows // 2)
            src = down_buf.at[s, part]
            dst = down_buf.at[s, part]
        return remote(src, dst, w_send.at[way, s, p], w_recv.at[s, p], dp=(line, pal)[way])

    def own_out(way, *ps):
        for p in ps:
            piece(me, p, way, True).start()

    def take(s, p, *out):
        piece(s, p, 0).wait_recv()
        for way in out:
            piece(s, p, way).start()

    for c in local[:2]:
        c.wait()
    for p in range(4):
        own_out(0, p)
        own_out(1, p)

    @pl.when(end)
    def _():
        for p in (4, 5):
            own_out(0, p)
            own_out(1, p)

    for c in local[2:]:
        c.wait()
    t_rows = tok_v.shape[0]
    topk = ids_v.shape[0]
    row = lax.broadcasted_iota(jnp.int32, (slots, t_rows), 0)
    row_e = row // PAD
    row_r = (row - row_e * PAD).astype(F32)
    idv = ids_v[...]
    scv = sc_v[...].astype(F32)
    live = jnp.zeros((slots, t_rows), F32)
    gcol = jnp.zeros((slots, t_rows), F32)
    hits = []
    for k in range(topk):
        hit = idv[k:k + 1, :] == row_e
        hits.append(hit)
        live = jnp.where(hit, 1.0, live)
        gcol = jnp.where(hit, scv[k:k + 1, :], gcol)
    upper = (lax.broadcasted_iota(jnp.int32, (t_rows, t_rows), 0)
             < lax.broadcasted_iota(jnp.int32, (t_rows, t_rows), 1))
    rank = dot(live.astype(BF), jnp.where(upper, 1.0, 0.0).astype(BF))
    pick_t = jnp.where(rank == row_r, live, 0.0)
    pick_b = pick_t.astype(BF)
    gate_col = jnp.sum(pick_t * gcol, axis=1, keepdims=True)

    def block(i):
        start = i * PAD
        return pl.ds(start if isinstance(i, int) else pl.multiple_of(start, PAD), PAD)

    outs, ins = (x_out, d_out), (x_in, d_in)

    def slots_to(kind, e, place):
        return remote(outs[kind].at[block(e), :], ins[kind].at[block(place * groups + mine), :],
                      s_send.at[kind, e], s_recv.at[kind, place, mine], dp=my_mid, expert=e)

    def slots_from(kind, place, e):
        return remote(outs[kind].at[block(e), :], ins[kind].at[block(place * groups + e), :],
                      s_send.at[kind, e], s_recv.at[kind, place, e], dp=my_mid, expert=e)

    def other(k):
        return lax.rem(mine + k, groups)

    def slots_out(kind):
        @pl.when(end)
        def _():
            for e in range(groups):
                slots_to(kind, e, 1).start()

        @pl.when(mid)
        def _():
            for k in range(1, groups):
                slots_to(kind, other(k), 0).start()
            ins[kind][block(mine), :] = outs[kind][block(mine), :]

    x_out[...] = dot(pick_b, tok_v[...]).astype(BF)
    slots_out(0)
    d_out[:, feats:] = jnp.broadcast_to(gate_col, (slots, LANES)).astype(BF)
    d_out[:, :feats] = (gate_col * dot(pick_b, dout_v[...])).astype(BF)

    @pl.when(end)
    def _():
        for p in range(4):
            take(pal, p, 0)

    slots_out(1)

    @pl.when(end)
    def _():
        for p in (4, 5):
            take(pal, p, 0)

    pick = jnp.transpose(pick_t).astype(BF)
    folded = [dot(pick, spread(groups, j, False)).astype(BF) for j in range(FOLD)]

    def dx_to(d):
        return remote(dx_send.at[d], dx_buf.at[2 * side + xi], x_send.at[d], x_recv.at[2 * side + xi], dp=d)

    def dx_from(q):
        return remote(dx_send.at[0], dx_buf.at[q], x_send.at[0], x_recv.at[q], dp=pal)

    def hid(q, d):
        return remote(hid_buf.at[q], hid_buf.at[q], h_send.at[q, d], h_recv.at[q], dp=d)

    rets, backs = (ret_a, ret_b), (back_a, back_b)

    def ret_to(part, place, e):
        return remote(rets[part].at[block(place * groups + e), :], backs[part].at[block(mine), :],
                      b_send.at[part, place, e], b_recv.at[part, mine], dp=(my_mid, my_end)[place], expert=e)

    def back_from(part, e):
        return remote(rets[part].at[block(e), :], backs[part].at[block(e), :],
                      b_send.at[part, 0, e], b_recv.at[part, e], dp=my_mid, expert=e)

    def ret_out(part):
        for e in range(groups):
            ret_to(part, 1, e).start()
        for k in range(1, groups):
            ret_to(part, 0, other(k)).start()
        backs[part][block(mine), :] = rets[part][block(mine), :]

    my_q, pal_q = 2 * side + xi, 2 * side + xo
    far_q, fpal_q = 2 - 2 * side + xi, 2 - 2 * side + xo
    a, b, c, d, e_, f, g = (my_end, at(xo, z_end), pal, far_mid, far_end, at(xo, z_far), at(xo, z_edge))

    @pl.when(mid)
    def _():
        many = 2 * slots
        packed = 2 * groups * CAP

        def cols(s):
            return pl.ds(pl.multiple_of(s * rows, LANES), rows)

        def add(s):
            pre_acc[...] += dot(x_in[:, cols(s)], gate_buf[s])

        def add_v(s):
            v_acc[...] += dot(d_in[:, cols(s)], down_buf[s])

        def slots_wait(kind):
            for k in range(1, groups):
                slots_from(kind, 0, other(k)).wait_recv()
            for e in range(groups):
                slots_from(kind, 1, e).wait_recv()

        take(a, 0, 0)
        take(a, 1, 0)
        take(d, 2, 1)
        take(a, 2, 0)
        take(d, 3, 1)
        take(a, 3, 0)
        take(c, 0, 0)
        take(c, 1, 0)
        own_out(0, 4, 5)
        take(a, 4, 0)
        take(a, 5, 0)
        for p in range(4):
            take(e_, p, 1)
        own_out(1, 4, 5)
        slots_wait(0)
        pre_acc[...] = dot(x_in[:, cols(me)], gate_buf[me])
        take(c, 2)
        take(c, 3)
        take(d, 0)
        take(d, 1)
        for s in (a, c, d, e_):
            add(s)
        def rest(s):
            for p in range(4):
                take(s, p)
            add(s)

        rest(f)
        take(c, 4, 0)
        rest(g)
        take(d, 5, 1)
        rest(b)

        pr = lax.broadcasted_iota(jnp.int32, (packed, many), 0)
        pc = lax.broadcasted_iota(jnp.int32, (packed, many), 1)
        pack = jnp.where(pc == (pr // CAP) * PAD + pr % CAP, 1.0, 0.0).astype(BF)
        pre = pre_acc[...]
        ga = pre[:, :width]
        gb = pre[:, width:]
        sig = jax.nn.sigmoid(ga)
        act = ga * sig
        slope = gb * sig * (1.0 + ga * (1.0 - sig))
        hidden = (act * gb).astype(BF)
        hid_buf[my_q] = dot(pack, hidden).astype(BF)
        hid(my_q, my_end).start()
        take(e_, 4, 1)
        take(e_, 5, 1)
        for s in (far_end, pal, far_mid):
            hid(my_q, s).start()

        slots_wait(1)
        dexp = dot(pack, d_in[:, :feats]).astype(BF)
        for s in range(n):
            dx_send[s] = dexp[:, s * rows:(s + 1) * rows]
        for s in (e_, g, a, b, d, f, c):
            dx_to(s).start()
        dx_buf[my_q] = dx_send[me]
        gates = d_in[:, feats:feats + 1].astype(F32)
        inverse = jnp.where(gates > 0.0, 1.0 / jnp.where(gates > 0.0, gates, 1.0), 0.0)
        v_acc[...] = dot(d_in[:, cols(me)], down_buf[me])
        take(c, 5)
        take(d, 4)
        for s in (a, c, d, e_):
            add_v(s)
        for s in (f, b, g):
            take(s, 4)
            take(s, 5)
            add_v(s)

        d_hid = v_acc[...]
        d_pre = jnp.concatenate([d_hid * slope, d_hid * act], axis=1).astype(BF)
        quarter = feats // 4

        def d_slot(j):
            w = gate_buf[j * n // 4:(j + 1) * n // 4].reshape(quarter, 2 * width)
            return dot(d_pre, w, ((1,), (1,)))

        last = d_slot(3).astype(BF)

        def fold(j):
            return (d_slot(j) + dot(spread(2 * groups, j, True), last)).astype(BF)

        ret_a[...] = fold(0)
        ret_out(0)
        for j in range(1, FOLD):
            ret_b[:, (j - 1) * quarter:j * quarter] = fold(j)
        slot_grad = jnp.sum(hidden.astype(F32) * d_hid, axis=1, keepdims=True) * inverse
        ret_b[:, 2 * quarter:] = jnp.broadcast_to(slot_grad, (many, LANES)).astype(BF)
        ret_out(1)

        hid(far_q, me).wait_recv()
        hid(far_q, pal).start()
        o_down[0] = dot(dx_buf[my_q], hid_buf[my_q], ((0,), (0,)))
        dx_from(far_q).wait_recv()
        o_down[0] += dot(dx_buf[far_q], hid_buf[far_q], ((0,), (0,)))

    @pl.when(end)
    def _():
        for q in (my_q, far_q):
            hid(q, me).wait_recv()
            hid(q, pal).start()
        dx_from(my_q).wait_recv()
        dx_from(far_q).wait_recv()
        o_down[0] = (dot(dx_buf[my_q], hid_buf[my_q], ((0,), (0,)))
                     + dot(dx_buf[far_q], hid_buf[far_q], ((0,), (0,))))

    def grow(q):
        hid(q, me).wait_recv()
        dx_from(q).wait_recv()
        o_down[0] += dot(dx_buf[q], hid_buf[q], ((0,), (0,)))

    grow(pal_q)
    quarter = feats // 4

    def back_wait(part):
        for k in range(1, groups):
            back_from(part, other(k)).wait_recv()
        pl.when(end)(lambda: back_from(part, mine).wait_recv())

    back_wait(0)
    o_tok[:, :quarter] = dot(pick, back_a[...]).astype(BF)
    last = dot(folded[0], back_a[...])
    grow(fpal_q)
    back_wait(1)
    for j in range(1, FOLD):
        part = back_b[:, (j - 1) * quarter:j * quarter]
        o_tok[:, j * quarter:(j + 1) * quarter] = dot(pick, part).astype(BF)
        last += dot(folded[j], part)
    o_tok[:, 3 * quarter:] = last.astype(BF)
    weighted = pick_t * back_b[:, 2 * quarter:2 * quarter + 1].astype(F32)
    o_gates[...] = jnp.concatenate(
        [jnp.sum(jnp.where(hit, weighted, 0.0), axis=0, keepdims=True) for hit in hits],
        axis=0).astype(BF)

    for p in range(6):
        for way in range(2):
            piece(me, p, way, True).wait_send()

    @pl.when(end)
    def _():
        for e in range(groups):
            slots_to(0, e, 1).wait_send()
            slots_to(1, e, 1).wait_send()
        for p in range(6):
            piece(pal, p, 0).wait_send()
        for q in (my_q, far_q):
            hid(q, pal).wait_send()

    @pl.when(mid)
    def _():
        for p in range(6):
            piece(a, p, 0).wait_send()
        for s, p, way in ((c, 0, 0), (c, 1, 0), (c, 4, 0), (d, 2, 1), (d, 3, 1), (d, 5, 1)):
            piece(s, p, way).wait_send()
        for p in range(6):
            piece(e_, p, 1).wait_send()
        for k in range(1, groups):
            slots_to(0, other(k), 0).wait_send()
            slots_to(1, other(k), 0).wait_send()
            for part in range(2):
                ret_to(part, 0, other(k)).wait_send()
        for e in range(groups):
            for part in range(2):
                ret_to(part, 1, e).wait_send()
        for s in (far_end, far_mid, my_end, pal):
            hid(my_q, s).wait_send()
        hid(far_q, pal).wait_send()
        for s in (a, b, c, d, e_, f, g):
            dx_to(s).wait_send()


def place(*refs):
    ins, outs, sem = refs[:3], refs[3:6], refs[6]
    copies = [pltpu.make_async_copy(src, dst, sem.at[i]) for i, (src, dst) in enumerate(zip(ins, outs))]
    for c in copies:
        c.start()
    for c in copies:
        c.wait()


def place_whole(*refs):
    for src, dst in zip(refs[:3], refs[3:]):
        dst[...] = src[...]


def solution(mesh):
    groups = mesh.shape["expert"]
    n = mesh.shape["dp"]
    inner = 1
    while n % (inner * 2) == 0 and (inner * 2) ** 2 <= n:
        inner *= 2
    outer = n // inner

    def on_device(tokens, d_output, expert_ids, gate_scores, gate_up_w, down_w):
        feats = tokens.shape[1]
        rows = gate_up_w.shape[1]
        width = down_w.shape[2]
        slots = groups * PAD
        packed = groups * CAP
        vmem = pl.BlockSpec(memory_space=pltpu.VMEM)
        dma = pltpu.SemaphoreType.DMA
        grads, d_gates, d_down = pl.pallas_call(
            functools.partial(ring_kernel, groups, outer, inner),
            out_shape=(
                jax.ShapeDtypeStruct(tokens.shape, BF),
                jax.ShapeDtypeStruct(gate_scores.shape[::-1], BF),
                jax.ShapeDtypeStruct(down_w.shape, F32),
            ),
            in_specs=[vmem] * 6,
            out_specs=(vmem,) * 3,
            scratch_shapes=[
                pltpu.VMEM((n, rows, 2 * width), BF),
                pltpu.VMEM((n, rows, width), BF),
                pltpu.VMEM((n, slots, rows), BF),
                pltpu.VMEM((n, slots, rows), BF),
                pltpu.VMEM((slots, 2 * width), F32),
                pltpu.VMEM((slots, width), F32),
                pltpu.VMEM((slots, 2 * feats + LANES), BF),
                pltpu.VMEM((slots, 2 * feats + LANES), BF),
                pltpu.VMEM((n, packed, width), BF),
                pltpu.VMEM((n, packed, rows), BF),
                pltpu.VMEM((n, packed, rows), BF),
                pltpu.VMEM((slots, feats + LANES), BF),
                pltpu.VMEM((slots, feats + LANES), BF),
                dma((2, 4, n)), dma((2, n)), dma((2,)),
                dma((groups,)), dma((groups,)),
                dma((n,)), dma((n,)),
                dma((n,)), dma((n,)),
                dma((groups,)), dma((groups,)),
            ],
            compiler_params=pltpu.CompilerParams(
                collective_id=0, has_side_effects=True, vmem_limit_bytes=60 * 2**20),
        )(tokens, d_output, expert_ids.T, gate_scores.T, gate_up_w, down_w)
        grads, d_gates, d_down = pl.pallas_call(
            place_whole,
            out_shape=tuple(jax.ShapeDtypeStruct(v.shape, v.dtype) for v in (grads, d_gates, d_down)),
            in_specs=[vmem] * 3,
            out_specs=(vmem,) * 3,
        )(grads, d_gates, d_down)
        return grads, d_gates.T, d_down

    def paired(tokens, d_output, expert_ids, gate_scores, gate_up_w, down_w):
        t_rows, feats = tokens.shape
        topk = expert_ids.shape[1]
        rows = gate_up_w.shape[1]
        width = down_w.shape[2]
        slots = groups * PAD
        packed = 2 * groups * CAP
        vmem = pl.BlockSpec(memory_space=pltpu.VMEM)
        hbm = pl.BlockSpec(memory_space=pltpu.HBM)
        dma = pltpu.SemaphoreType.DMA
        shapes = (
            jax.ShapeDtypeStruct(tokens.shape, BF),
            jax.ShapeDtypeStruct(gate_scores.shape[::-1], BF),
            jax.ShapeDtypeStruct(down_w.shape, F32),
        )
        parts = pl.pallas_call(
            functools.partial(mid_kernel, groups),
            out_shape=shapes,
            in_specs=[hbm] * 6,
            out_specs=(vmem,) * 3,
            scratch_shapes=[
                pltpu.VMEM((n, rows, 2 * width), BF),
                pltpu.VMEM((n, rows, width), BF),
                pltpu.VMEM((t_rows, feats), BF),
                pltpu.VMEM((t_rows, feats), BF),
                pltpu.VMEM((topk, t_rows), jnp.int32),
                pltpu.VMEM((topk, t_rows), BF),
                pltpu.VMEM((slots, feats), BF),
                pltpu.VMEM((slots, feats + LANES), BF),
                pltpu.VMEM((2 * slots, feats), BF),
                pltpu.VMEM((2 * slots, feats + LANES), BF),
                pltpu.VMEM((2 * slots, 2 * width), F32),
                pltpu.VMEM((2 * slots, width), F32),
                pltpu.VMEM((n, packed, rows), BF),
                pltpu.VMEM((4, packed, rows), BF),
                pltpu.VMEM((4, packed, width), BF),
                pltpu.VMEM((2 * slots, feats // 4), BF),
                pltpu.VMEM((2 * slots, feats // 2 + LANES), BF),
                pltpu.VMEM((slots, feats // 4), BF),
                pltpu.VMEM((slots, feats // 2 + LANES), BF),
                dma((6,)),
                dma((2, n, 6)), dma((n, 6)),
                dma((2, groups)), dma((2, 2, groups)),
                dma((n,)), dma((4,)),
                dma((4, n)), dma((4,)),
                dma((2, 2, groups)), dma((2, groups)),
            ],
            compiler_params=pltpu.CompilerParams(
                collective_id=0, has_side_effects=True, vmem_limit_bytes=16 * 2**20),
        )(*(pltpu.with_memory_space_constraint(v, pltpu.HBM) for v in (
            gate_up_w, down_w, tokens, d_output, expert_ids.T, gate_scores.T)))
        grads, d_gates, d_down = pl.pallas_call(
            place,
            out_shape=shapes,
            in_specs=[vmem] * 3,
            out_specs=(hbm,) * 3,
            scratch_shapes=[dma((3,))],
            compiler_params=pltpu.CompilerParams(vmem_limit_bytes=2**20),
        )(*parts)
        return grads, d_gates.T, d_down

    lines = inner == 2 and outer == 4
    tok = P(("expert", "dp"), None)
    w = P("expert", "dp", None)
    return jax.shard_map(
        paired if lines else on_device, mesh=mesh, in_specs=(tok, tok, tok, tok, w, w),
        out_specs=(tok, tok, w), check_vma=False)
```

```python
import functools

import jax
import jax.numpy as jnp
from jax import lax
from jax.experimental import pallas as pl
from jax.experimental.pallas import tpu as pltpu
from jax.sharding import PartitionSpec as P

CAP = 12
PAD = 16
LANES = 128
FOLD = CAP // (PAD - CAP)
BF = jnp.bfloat16
F32 = jnp.float32


def dot(left, right, dims=((1,), (0,))):
    return lax.dot_general(left, right, (dims, ((), ())), preferred_element_type=F32)


def ring_kernel(groups, outer, inner, tok, dout, ids, scores, gate_in, down_in,
           o_tok, o_gates, o_down,
           gate_buf, down_buf, x_ch, up_ch, pre_acc, u_acc, send, recv, hid_buf, dx_send, dx_buf, ret, back,
           w_send, w_recv, own_sem, s_send, s_recv, h_send, h_recv, x_send, x_recv, b_send, b_recv):
    n = outer * inner
    me = lax.axis_index("dp")
    mine = lax.axis_index("expert")
    zo = me // inner
    xi = me - zo * inner
    slots = groups * PAD
    rows = gate_in.shape[1]
    feats = tok.shape[1]
    width = down_in.shape[2]
    ins = (down_in, gate_in)
    bufs = (down_buf, gate_buf)

    barrier = pltpu.get_barrier_semaphore()
    for k in range(1, n):
        pl.semaphore_signal(barrier, inc=1, device_id={"dp": lax.rem(me + k, n)},
                            device_id_type=pl.DeviceIdType.MESH)
    for k in range(1, groups):
        pl.semaphore_signal(barrier, inc=1, device_id={"expert": lax.rem(mine + k, groups)},
                            device_id_type=pl.DeviceIdType.MESH)
    pl.semaphore_wait(barrier, n - 1 + groups - 1)

    def remote(src, dst, ss, rs, **where):
        return pltpu.make_async_remote_copy(
            src_ref=src, dst_ref=dst, send_sem=ss, recv_sem=rs,
            device_id=where, device_id_type=pl.DeviceIdType.MESH)

    def target(way):
        return me + (inner, -inner, 1, -1)[way]

    def can(way):
        return (zo < outer - 1, zo > 0, xi < inner - 1, xi > 0)[way]

    def hop(w, s, way, own=False):
        src = ins[w].at[0] if own else bufs[w].at[s]
        return remote(src, bufs[w].at[s], w_send.at[w, way, s], w_recv.at[w, s], dp=target(way))

    started = []
    accs = (u_acc, pre_acc)
    chunks = (up_ch, x_ch)

    def forward(w, s, way, valid, own=False):
        ok = can(way) if valid is None else jnp.logical_and(can(way), valid)

        @pl.when(ok)
        def _():
            hop(w, s, way, own).start()
        started.append((ok, w, s, way, own))

    def arrive(w, s, valid):
        @pl.when(valid)
        def _():
            hop(w, s, 0).wait_recv()

    def add(w, s, valid):
        @pl.when(valid)
        def _():
            accs[w][...] += dot(chunks[w][s], bufs[w][s])

    def outer_shards(d):
        return ((0, me - d * inner, zo >= d), (1, me + d * inner, zo + d < outer))

    def outer_step(w, d):
        for way, s, valid in outer_shards(d):
            arrive(w, s, valid)
            for go in (way, 2, 3):
                forward(w, s, go, valid)

    def outer_add(w, d):
        for _, s, valid in outer_shards(d):
            add(w, s, valid)

    def inner_step(w, d):
        for di in range(1, inner):
            for sign in ((1,) if d == 0 else (-1, 1)):
                so = zo + sign * d
                good = jnp.logical_and(so >= 0, so < outer)
                for way, step in ((2, -di), (3, di)):
                    xs = xi + step
                    valid = jnp.logical_and(good, jnp.logical_and(xs >= 0, xs < inner))
                    s = so * inner + xs
                    arrive(w, s, valid)
                    if inner > 2:
                        forward(w, s, way, valid)
                    add(w, s, valid)

    own = [pltpu.make_async_copy(ins[w].at[0], bufs[w].at[me], own_sem.at[w]) for w in range(2)]
    for way in range(4):
        forward(1, me, way, None, own=True)
    for way in range(4):
        forward(0, me, way, None, own=True)
    for c in own:
        c.start()

    t_rows = tok.shape[0]
    topk = ids.shape[0]
    row = lax.broadcasted_iota(jnp.int32, (slots, t_rows), 0)
    row_e = row // PAD
    row_r = (row - row_e * PAD).astype(F32)
    idv = ids[...]
    scv = scores[...].astype(F32)
    live = jnp.zeros((slots, t_rows), F32)
    gcol = jnp.zeros((slots, t_rows), F32)
    hits = []
    for k in range(topk):
        hit = idv[k:k + 1, :] == row_e
        hits.append(hit)
        live = jnp.where(hit, 1.0, live)
        gcol = jnp.where(hit, scv[k:k + 1, :], gcol)
    upper = (lax.broadcasted_iota(jnp.int32, (t_rows, t_rows), 0)
             < lax.broadcasted_iota(jnp.int32, (t_rows, t_rows), 1))
    rank = dot(live.astype(BF), jnp.where(upper, 1.0, 0.0).astype(BF))
    pick_t = jnp.where(rank == row_r, live, 0.0)
    pick_b = pick_t.astype(BF)
    send[:, 2 * feats:] = jnp.broadcast_to(
        jnp.sum(pick_t * gcol, axis=1, keepdims=True), (slots, LANES)).astype(BF)
    send[:, :feats] = dot(pick_b, tok[...]).astype(BF)
    send[:, feats:2 * feats] = dot(pick_b, dout[...]).astype(BF)

    def block(e):
        return pl.ds(pl.multiple_of(e * PAD, PAD), PAD)

    def swap(src, dst, ss, rs, k):
        e = lax.rem(mine + k, groups)
        return remote(src.at[block(e), :], dst.at[block(mine), :], ss.at[k], rs.at[k], expert=e)

    for k in range(1, groups):
        swap(send, recv, s_send, s_recv, k).start()
    recv[block(mine), :] = send[block(mine), :]
    pick = jnp.transpose(pick_t).astype(BF)

    def peer(src, dst, ss, rs, k, sliced):
        d = lax.rem(me + k, n)
        return remote(src.at[d] if sliced else src.at[me], dst.at[me], ss.at[k], rs.at[k], dp=d)

    if outer > 1:
        outer_step(1, 1)
        outer_step(0, 1)

    packed = groups * CAP
    pr = lax.broadcasted_iota(jnp.int32, (packed, slots), 0)
    pc = lax.broadcasted_iota(jnp.int32, (packed, slots), 1)
    pack = jnp.where(pc == (pr // CAP) * PAD + pr % CAP, 1.0, 0.0).astype(BF)

    for k in range(1, groups):
        swap(send, recv, s_send, s_recv, k).wait_recv()
    gates = recv[:, 2 * feats:2 * feats + 1].astype(F32)
    upstream = recv[:, feats:2 * feats]
    dexp = dot(pack, (gates * upstream.astype(F32)).astype(BF)).astype(BF)
    for d in range(n):
        dx_send[d] = dexp[:, d * rows:(d + 1) * rows]
        x_ch[d] = recv[:, d * rows:(d + 1) * rows]
        up_ch[d] = recv[:, feats + d * rows:feats + (d + 1) * rows]
    for k in range(1, n):
        peer(dx_send, dx_buf, x_send, x_recv, k, True).start()
    dx_buf[me] = dx_send[me]
    pre_acc[...] = dot(x_ch[me], gate_in[0])
    u_acc[...] = dot(up_ch[me], down_in[0])

    for d in range(2, outer):
        outer_step(1, d)
        outer_step(0, d)
        outer_add(1, d - 1)
        outer_add(0, d - 1)
    for d in range(outer - 1):
        inner_step(1, d)
        inner_step(0, d)
    if outer > 1:
        outer_add(1, outer - 1)
        outer_add(0, outer - 1)
    inner_step(1, outer - 1)

    pre = pre_acc[...]
    a = pre[:, :width]
    b = pre[:, width:]
    sig = jax.nn.sigmoid(a)
    act = a * sig
    hidden = (act * b).astype(BF)
    hid_buf[me] = dot(pack, hidden).astype(BF)
    for k in range(1, n):
        peer(hid_buf, hid_buf, h_send, h_recv, k, False).start()

    inner_step(0, outer - 1)
    for c in own:
        c.wait()

    u = u_acc[...]
    d_hid = gates * u
    d_pre = jnp.concatenate(
        [d_hid * b * sig * (1.0 + a * (1.0 - sig)), d_hid * act], axis=1).astype(BF)
    gate_full = gate_buf[...].reshape(n * rows, 2 * width)
    ret[:, feats:] = jnp.broadcast_to(
        jnp.sum(hidden.astype(F32) * u, axis=1, keepdims=True), (slots, LANES)).astype(BF)
    ret[:, :feats] = dot(d_pre, gate_full, ((1,), (1,))).astype(BF)
    for k in range(1, groups):
        swap(ret, back, b_send, b_recv, k).start()
    back[block(mine), :] = ret[block(mine), :]

    o_down[0] = dot(dx_buf[me], hid_buf[me], ((0,), (0,)))
    for k in range(1, n):
        s = lax.rem(me - k + n, n)
        peer(dx_send, dx_buf, x_send, x_recv, k, True).wait_recv()
        peer(hid_buf, hid_buf, h_send, h_recv, k, False).wait_recv()
        o_down[0] += dot(dx_buf[s], hid_buf[s], ((0,), (0,)))

    for k in range(1, groups):
        swap(ret, back, b_send, b_recv, k).wait_recv()
    o_tok[...] = dot(pick, back[:, :feats]).astype(BF)
    weighted = pick_t * back[:, feats:feats + 1].astype(F32)
    o_gates[...] = jnp.concatenate(
        [jnp.sum(jnp.where(hit, weighted, 0.0), axis=0, keepdims=True) for hit in hits],
        axis=0).astype(BF)

    for ok, w, s, way, is_own in started:
        @pl.when(ok)
        def _(w=w, s=s, way=way, is_own=is_own):
            hop(w, s, way, is_own).wait_send()
    for k in range(1, groups):
        swap(send, recv, s_send, s_recv, k).wait_send()
        swap(ret, back, b_send, b_recv, k).wait_send()
    for k in range(1, n):
        peer(dx_send, dx_buf, x_send, x_recv, k, True).wait_send()
        peer(hid_buf, hid_buf, h_send, h_recv, k, False).wait_send()

def remote(src, dst, ss, rs, **where):
    return pltpu.make_async_remote_copy(
        src_ref=src, dst_ref=dst, send_sem=ss, recv_sem=rs,
        device_id=where, device_id_type=pl.DeviceIdType.MESH)


def spread(blocks, j, down):
    size = blocks * PAD
    r = lax.broadcasted_iota(jnp.int32, (size, size), 0)
    c = lax.broadcasted_iota(jnp.int32, (size, size), 1)
    if not down:
        r, c = c, r
    i = r % PAD - CAP
    hit = jnp.logical_and(jnp.logical_and(r // PAD == c // PAD, i >= 0), c % PAD == FOLD * i + j)
    return jnp.where(hit, 1.0, 0.0).astype(BF)


def mid_kernel(groups, gate_in, down_in, tok_in, dout_in, ids_in, sc_in,
               o_tok, o_gates, o_down,
               gate_buf, down_buf, tok_v, dout_v, ids_v, sc_v, x_out, d_out, x_in, d_in, pre_acc, v_acc,
               dx_send, dx_buf, hid_buf, ret_a, ret_b, back_a, back_b,
               l_sem, w_send, w_recv, s_send, s_recv, x_send, x_recv,
               h_send, h_recv, b_send, b_recv):
    me = lax.axis_index("dp")
    mine = lax.axis_index("expert")
    zo = me // 2
    xi = me - 2 * zo
    side = zo // 2
    mid = jnp.logical_or(zo == 1, zo == 2)
    end = jnp.logical_not(mid)
    slots = groups * PAD
    rows = gate_in.shape[1]
    feats = tok_in.shape[1]
    width = down_in.shape[2]
    n = feats // rows

    def at(x, z):
        return 2 * z + x

    xo = 1 - xi
    pal = at(xo, zo)
    z_mid, z_end, z_far, z_edge = 1 + side, 3 * side, 2 - side, 3 - 3 * side
    my_mid, my_end = at(xi, z_mid), at(xi, z_end)
    far_mid, far_end = at(xi, z_far), at(xi, z_edge)
    line = jnp.where(mid, far_mid, my_mid)

    barrier = pltpu.get_barrier_semaphore()

    def greet(**where):
        pl.semaphore_signal(barrier, inc=1, device_id=where, device_id_type=pl.DeviceIdType.MESH)

    greet(dp=pal)

    @pl.when(mid)
    def _():
        greet(dp=far_mid)
        for e in range(groups):
            greet(dp=my_end, expert=e)
        for k in range(1, groups):
            greet(expert=lax.rem(mine + k, groups))

    local = [pltpu.make_async_copy(src, dst, l_sem.at[i]) for i, (src, dst) in enumerate((
        (gate_in.at[0], gate_buf.at[me]), (down_in.at[0], down_buf.at[me]),
        (ids_in, ids_v), (sc_in, sc_v), (tok_in, tok_v), (dout_in, dout_v)))]
    for c in local:
        c.start()
    pl.semaphore_wait(barrier, 1 + groups)

    def piece(s, p, way, own=False):
        if p < 4:
            part = pl.ds(p * (rows // 4), rows // 4)
            src = gate_buf.at[s, part]
            dst = gate_buf.at[s, part]
        else:
            part = pl.ds((p - 4) * (rows // 2), rows // 2)
            src = down_buf.at[s, part]
            dst = down_buf.at[s, part]
        return remote(src, dst, w_send.at[way, s, p], w_recv.at[s, p], dp=(line, pal)[way])

    def own_out(way, *ps):
        for p in ps:
            piece(me, p, way, True).start()

    def take(s, p, *out):
        piece(s, p, 0).wait_recv()
        for way in out:
            piece(s, p, way).start()

    for c in local[:2]:
        c.wait()
    for p in range(4):
        own_out(0, p)
        own_out(1, p)

    @pl.when(end)
    def _():
        for p in (4, 5):
            own_out(0, p)
            own_out(1, p)

    for c in local[2:]:
        c.wait()
    t_rows = tok_v.shape[0]
    topk = ids_v.shape[0]
    row = lax.broadcasted_iota(jnp.int32, (slots, t_rows), 0)
    row_e = row // PAD
    row_r = (row - row_e * PAD).astype(F32)
    idv = ids_v[...]
    scv = sc_v[...].astype(F32)
    live = jnp.zeros((slots, t_rows), F32)
    gcol = jnp.zeros((slots, t_rows), F32)
    hits = []
    for k in range(topk):
        hit = idv[k:k + 1, :] == row_e
        hits.append(hit)
        live = jnp.where(hit, 1.0, live)
        gcol = jnp.where(hit, scv[k:k + 1, :], gcol)
    upper = (lax.broadcasted_iota(jnp.int32, (t_rows, t_rows), 0)
             < lax.broadcasted_iota(jnp.int32, (t_rows, t_rows), 1))
    rank = dot(live.astype(BF), jnp.where(upper, 1.0, 0.0).astype(BF))
    pick_t = jnp.where(rank == row_r, live, 0.0)
    pick_b = pick_t.astype(BF)
    gate_col = jnp.sum(pick_t * gcol, axis=1, keepdims=True)

    def block(i):
        start = i * PAD
        return pl.ds(start if isinstance(i, int) else pl.multiple_of(start, PAD), PAD)

    outs, ins = (x_out, d_out), (x_in, d_in)
    quarter = feats // 4
    sent_cols = (pl.ds(0, 3 * quarter), pl.ds(0, LANES + 3 * quarter))

    def fold_in(kind, whole):
        base = kind * LANES
        behind = whole[:, 3 * quarter:]
        for j in range(FOLD):
            part = whole[:, j * quarter:(j + 1) * quarter].astype(F32) + dot(spread(groups, j, True), behind)
            outs[kind][:, base + j * quarter:base + (j + 1) * quarter] = part.astype(BF)

    def unfold(kind):
        base = kind * LANES
        tail = sum(dot(spread(2 * groups, j, False), ins[kind][:, base + j * quarter:base + (j + 1) * quarter])
                   for j in range(FOLD))
        ins[kind][:, base + 3 * quarter:base + feats] = tail.astype(BF)

    def slots_to(kind, e, place):
        return remote(outs[kind].at[block(e), :], ins[kind].at[block(place * groups + mine), sent_cols[kind]],
                      s_send.at[kind, e], s_recv.at[kind, place, mine], dp=my_mid, expert=e)

    def slots_from(kind, place, e):
        return remote(outs[kind].at[block(e), :], ins[kind].at[block(place * groups + e), sent_cols[kind]],
                      s_send.at[kind, e], s_recv.at[kind, place, e], dp=my_mid, expert=e)

    def other(k):
        return lax.rem(mine + k, groups)

    def slots_out(kind):
        @pl.when(end)
        def _():
            for e in range(groups):
                slots_to(kind, e, 1).start()

        @pl.when(mid)
        def _():
            for k in range(1, groups):
                slots_to(kind, other(k), 0).start()
            ins[kind][block(mine), sent_cols[kind]] = outs[kind][block(mine), :]

    fold_in(0, dot(pick_b, tok_v[...]).astype(BF))
    slots_out(0)
    d_out[:, :LANES] = jnp.broadcast_to(gate_col, (slots, LANES)).astype(BF)
    fold_in(1, (gate_col * dot(pick_b, dout_v[...])).astype(BF))

    @pl.when(end)
    def _():
        for p in range(4):
            take(pal, p, 0)

    slots_out(1)

    @pl.when(end)
    def _():
        for p in (4, 5):
            take(pal, p, 0)

    pick = jnp.transpose(pick_t).astype(BF)
    folded = [dot(pick, spread(groups, j, False)).astype(BF) for j in range(FOLD)]

    def dx_to(d):
        return remote(dx_send.at[d], dx_buf.at[2 * side + xi], x_send.at[d], x_recv.at[2 * side + xi], dp=d)

    def dx_from(q):
        return remote(dx_send.at[0], dx_buf.at[q], x_send.at[0], x_recv.at[q], dp=pal)

    def hid(q, d):
        return remote(hid_buf.at[q], hid_buf.at[q], h_send.at[q, d], h_recv.at[q], dp=d)

    rets, backs = (ret_a, ret_b), (back_a, back_b)

    def ret_to(part, place, e):
        return remote(rets[part].at[block(place * groups + e), :], backs[part].at[block(mine), :],
                      b_send.at[part, place, e], b_recv.at[part, mine], dp=(my_mid, my_end)[place], expert=e)

    def back_from(part, e):
        return remote(rets[part].at[block(e), :], backs[part].at[block(e), :],
                      b_send.at[part, 0, e], b_recv.at[part, e], dp=my_mid, expert=e)

    def ret_out(part):
        for e in range(groups):
            ret_to(part, 1, e).start()
        for k in range(1, groups):
            ret_to(part, 0, other(k)).start()
        backs[part][block(mine), :] = rets[part][block(mine), :]

    my_q, pal_q = 2 * side + xi, 2 * side + xo
    far_q, fpal_q = 2 - 2 * side + xi, 2 - 2 * side + xo
    a, b, c, d, e_, f, g = (my_end, at(xo, z_end), pal, far_mid, far_end, at(xo, z_far), at(xo, z_edge))

    @pl.when(mid)
    def _():
        many = 2 * slots
        packed = 2 * groups * CAP

        def cols(s, base=0):
            return pl.ds(pl.multiple_of(base + s * rows, LANES), rows)

        def add(s):
            pre_acc[...] += dot(x_in[:, cols(s)], gate_buf[s])

        def add_v(s):
            v_acc[...] += dot(d_in[:, cols(s, LANES)], down_buf[s])

        def slots_wait(kind):
            for k in range(1, groups):
                slots_from(kind, 0, other(k)).wait_recv()
            for e in range(groups):
                slots_from(kind, 1, e).wait_recv()
            unfold(kind)

        take(a, 0, 0)
        take(a, 1, 0)
        take(d, 2, 1)
        take(a, 2, 0)
        take(d, 3, 1)
        take(a, 3, 0)
        take(c, 0, 0)
        take(c, 1, 0)
        own_out(0, 4, 5)
        take(a, 4, 0)
        take(a, 5, 0)
        for p in range(4):
            take(e_, p, 1)
        own_out(1, 4, 5)
        slots_wait(0)
        pre_acc[...] = dot(x_in[:, cols(me)], gate_buf[me])
        take(c, 2)
        take(c, 3)
        take(d, 0)
        take(d, 1)
        for s in (a, c, d, e_):
            add(s)
        def rest(s):
            for p in range(4):
                take(s, p)
            add(s)

        rest(f)
        rest(g)
        rest(b)

        pr = lax.broadcasted_iota(jnp.int32, (packed, many), 0)
        pc = lax.broadcasted_iota(jnp.int32, (packed, many), 1)
        pack = jnp.where(pc == (pr // CAP) * PAD + pr % CAP, 1.0, 0.0).astype(BF)
        pre = pre_acc[...]
        ga = pre[:, :width]
        gb = pre[:, width:]
        sig = jax.nn.sigmoid(ga)
        act = ga * sig
        slope = gb * sig * (1.0 + ga * (1.0 - sig))
        hidden = (act * gb).astype(BF)
        hid_buf[my_q] = dot(pack, hidden).astype(BF)
        hid(my_q, my_end).start()
        hid(my_q, far_end).start()
        take(c, 4, 0)
        take(d, 5, 1)
        take(e_, 4, 1)
        take(e_, 5, 1)
        for s in (pal, far_mid):
            hid(my_q, s).start()

        slots_wait(1)
        dexp = dot(pack, d_in[:, LANES:]).astype(BF)
        for s in range(n):
            dx_send[s] = dexp[:, s * rows:(s + 1) * rows]
        for s in (e_, g, a, b, d, f, c):
            dx_to(s).start()
        dx_buf[my_q] = dx_send[me]
        gates = d_in[:, :1].astype(F32)
        inverse = jnp.where(gates > 0.0, 1.0 / jnp.where(gates > 0.0, gates, 1.0), 0.0)
        v_acc[...] = dot(d_in[:, cols(me, LANES)], down_buf[me])
        take(c, 5)
        take(d, 4)
        for s in (a, c, d, e_):
            add_v(s)
        for s in (f, b, g):
            take(s, 4)
            take(s, 5)
            add_v(s)

        used = lax.broadcasted_iota(jnp.int32, (many, width), 0) % PAD < CAP
        d_hid = jnp.where(used, v_acc[...], 0.0)
        d_pre = jnp.concatenate([d_hid * slope, d_hid * act], axis=1).astype(BF)
        quarter = feats // 4

        def d_slot(j):
            w = gate_buf[j * n // 4:(j + 1) * n // 4].reshape(quarter, 2 * width)
            return dot(d_pre, w, ((1,), (1,)))

        last = d_slot(3).astype(BF)

        def fold(j):
            return (d_slot(j) + dot(spread(2 * groups, j, True), last)).astype(BF)

        ret_a[...] = fold(0)
        ret_out(0)
        for j in range(1, FOLD):
            ret_b[:, (j - 1) * quarter:j * quarter] = fold(j)
        slot_grad = jnp.sum(hidden.astype(F32) * d_hid, axis=1, keepdims=True) * inverse
        ret_b[:, 2 * quarter:] = jnp.broadcast_to(slot_grad, (many, LANES)).astype(BF)
        ret_out(1)

        hid(far_q, me).wait_recv()
        hid(far_q, pal).start()
        o_down[0] = dot(dx_buf[my_q], hid_buf[my_q], ((0,), (0,)))
        dx_from(far_q).wait_recv()
        o_down[0] += dot(dx_buf[far_q], hid_buf[far_q], ((0,), (0,)))

    @pl.when(end)
    def _():
        for q in (my_q, far_q):
            hid(q, me).wait_recv()
            hid(q, pal).start()
        dx_from(my_q).wait_recv()
        dx_from(far_q).wait_recv()
        o_down[0] = (dot(dx_buf[my_q], hid_buf[my_q], ((0,), (0,)))
                     + dot(dx_buf[far_q], hid_buf[far_q], ((0,), (0,))))

    def grow(q):
        hid(q, me).wait_recv()
        dx_from(q).wait_recv()
        o_down[0] += dot(dx_buf[q], hid_buf[q], ((0,), (0,)))

    grow(pal_q)
    quarter = feats // 4

    def back_wait(part):
        for k in range(1, groups):
            back_from(part, other(k)).wait_recv()
        pl.when(end)(lambda: back_from(part, mine).wait_recv())

    back_wait(0)
    o_tok[:, :quarter] = dot(pick, back_a[...]).astype(BF)
    last = dot(folded[0], back_a[...])
    grow(fpal_q)
    back_wait(1)
    for j in range(1, FOLD):
        part = back_b[:, (j - 1) * quarter:j * quarter]
        o_tok[:, j * quarter:(j + 1) * quarter] = dot(pick, part).astype(BF)
        last += dot(folded[j], part)
    o_tok[:, 3 * quarter:] = last.astype(BF)
    weighted = pick_t * back_b[:, 2 * quarter:2 * quarter + 1].astype(F32)
    o_gates[...] = jnp.concatenate(
        [jnp.sum(jnp.where(hit, weighted, 0.0), axis=0, keepdims=True) for hit in hits],
        axis=0).astype(BF)

    for p in range(6):
        for way in range(2):
            piece(me, p, way, True).wait_send()

    @pl.when(end)
    def _():
        for e in range(groups):
            slots_to(0, e, 1).wait_send()
            slots_to(1, e, 1).wait_send()
        for p in range(6):
            piece(pal, p, 0).wait_send()
        for q in (my_q, far_q):
            hid(q, pal).wait_send()

    @pl.when(mid)
    def _():
        for p in range(6):
            piece(a, p, 0).wait_send()
        for s, p, way in ((c, 0, 0), (c, 1, 0), (c, 4, 0), (d, 2, 1), (d, 3, 1), (d, 5, 1)):
            piece(s, p, way).wait_send()
        for p in range(6):
            piece(e_, p, 1).wait_send()
        for k in range(1, groups):
            slots_to(0, other(k), 0).wait_send()
            slots_to(1, other(k), 0).wait_send()
            for part in range(2):
                ret_to(part, 0, other(k)).wait_send()
        for e in range(groups):
            for part in range(2):
                ret_to(part, 1, e).wait_send()
        for s in (far_end, far_mid, my_end, pal):
            hid(my_q, s).wait_send()
        hid(far_q, pal).wait_send()
        for s in (a, b, c, d, e_, f, g):
            dx_to(s).wait_send()


def place(*refs):
    ins, outs, sem = refs[:3], refs[3:6], refs[6]
    copies = [pltpu.make_async_copy(src, dst, sem.at[i]) for i, (src, dst) in enumerate(zip(ins, outs))]
    for c in copies:
        c.start()
    for c in copies:
        c.wait()


def place_whole(*refs):
    for src, dst in zip(refs[:3], refs[3:]):
        dst[...] = src[...]


def solution(mesh):
    groups = mesh.shape["expert"]
    n = mesh.shape["dp"]
    inner = 1
    while n % (inner * 2) == 0 and (inner * 2) ** 2 <= n:
        inner *= 2
    outer = n // inner

    def on_device(tokens, d_output, expert_ids, gate_scores, gate_up_w, down_w):
        feats = tokens.shape[1]
        rows = gate_up_w.shape[1]
        width = down_w.shape[2]
        slots = groups * PAD
        packed = groups * CAP
        vmem = pl.BlockSpec(memory_space=pltpu.VMEM)
        dma = pltpu.SemaphoreType.DMA
        grads, d_gates, d_down = pl.pallas_call(
            functools.partial(ring_kernel, groups, outer, inner),
            out_shape=(
                jax.ShapeDtypeStruct(tokens.shape, BF),
                jax.ShapeDtypeStruct(gate_scores.shape[::-1], BF),
                jax.ShapeDtypeStruct(down_w.shape, F32),
            ),
            in_specs=[vmem] * 6,
            out_specs=(vmem,) * 3,
            scratch_shapes=[
                pltpu.VMEM((n, rows, 2 * width), BF),
                pltpu.VMEM((n, rows, width), BF),
                pltpu.VMEM((n, slots, rows), BF),
                pltpu.VMEM((n, slots, rows), BF),
                pltpu.VMEM((slots, 2 * width), F32),
                pltpu.VMEM((slots, width), F32),
                pltpu.VMEM((slots, 2 * feats + LANES), BF),
                pltpu.VMEM((slots, 2 * feats + LANES), BF),
                pltpu.VMEM((n, packed, width), BF),
                pltpu.VMEM((n, packed, rows), BF),
                pltpu.VMEM((n, packed, rows), BF),
                pltpu.VMEM((slots, feats + LANES), BF),
                pltpu.VMEM((slots, feats + LANES), BF),
                dma((2, 4, n)), dma((2, n)), dma((2,)),
                dma((groups,)), dma((groups,)),
                dma((n,)), dma((n,)),
                dma((n,)), dma((n,)),
                dma((groups,)), dma((groups,)),
            ],
            compiler_params=pltpu.CompilerParams(
                collective_id=0, has_side_effects=True, vmem_limit_bytes=60 * 2**20),
        )(tokens, d_output, expert_ids.T, gate_scores.T, gate_up_w, down_w)
        grads, d_gates, d_down = pl.pallas_call(
            place_whole,
            out_shape=tuple(jax.ShapeDtypeStruct(v.shape, v.dtype) for v in (grads, d_gates, d_down)),
            in_specs=[vmem] * 3,
            out_specs=(vmem,) * 3,
        )(grads, d_gates, d_down)
        return grads, d_gates.T, d_down

    def paired(tokens, d_output, expert_ids, gate_scores, gate_up_w, down_w):
        t_rows, feats = tokens.shape
        topk = expert_ids.shape[1]
        rows = gate_up_w.shape[1]
        width = down_w.shape[2]
        slots = groups * PAD
        packed = 2 * groups * CAP
        vmem = pl.BlockSpec(memory_space=pltpu.VMEM)
        hbm = pl.BlockSpec(memory_space=pltpu.HBM)
        dma = pltpu.SemaphoreType.DMA
        shapes = (
            jax.ShapeDtypeStruct(tokens.shape, BF),
            jax.ShapeDtypeStruct(gate_scores.shape[::-1], BF),
            jax.ShapeDtypeStruct(down_w.shape, F32),
        )
        parts = pl.pallas_call(
            functools.partial(mid_kernel, groups),
            out_shape=shapes,
            in_specs=[hbm] * 6,
            out_specs=(vmem,) * 3,
            scratch_shapes=[
                pltpu.VMEM((n, rows, 2 * width), BF),
                pltpu.VMEM((n, rows, width), BF),
                pltpu.VMEM((t_rows, feats), BF),
                pltpu.VMEM((t_rows, feats), BF),
                pltpu.VMEM((topk, t_rows), jnp.int32),
                pltpu.VMEM((topk, t_rows), BF),
                pltpu.VMEM((slots, feats // 4 * 3), BF),
                pltpu.VMEM((slots, feats // 4 * 3 + LANES), BF),
                pltpu.VMEM((2 * slots, feats), BF),
                pltpu.VMEM((2 * slots, feats + LANES), BF),
                pltpu.VMEM((2 * slots, 2 * width), F32),
                pltpu.VMEM((2 * slots, width), F32),
                pltpu.VMEM((n, packed, rows), BF),
                pltpu.VMEM((4, packed, rows), BF),
                pltpu.VMEM((4, packed, width), BF),
                pltpu.VMEM((2 * slots, feats // 4), BF),
                pltpu.VMEM((2 * slots, feats // 2 + LANES), BF),
                pltpu.VMEM((slots, feats // 4), BF),
                pltpu.VMEM((slots, feats // 2 + LANES), BF),
                dma((6,)),
                dma((2, n, 6)), dma((n, 6)),
                dma((2, groups)), dma((2, 2, groups)),
                dma((n,)), dma((4,)),
                dma((4, n)), dma((4,)),
                dma((2, 2, groups)), dma((2, groups)),
            ],
            compiler_params=pltpu.CompilerParams(
                collective_id=0, has_side_effects=True, vmem_limit_bytes=16 * 2**20),
        )(*(pltpu.with_memory_space_constraint(v, pltpu.HBM) for v in (
            gate_up_w, down_w, tokens, d_output, expert_ids.T, gate_scores.T)))
        grads, d_gates, d_down = pl.pallas_call(
            place,
            out_shape=shapes,
            in_specs=[vmem] * 3,
            out_specs=(hbm,) * 3,
            scratch_shapes=[dma((3,))],
            compiler_params=pltpu.CompilerParams(vmem_limit_bytes=2**20),
        )(*parts)
        return grads, d_gates.T, d_down

    lines = inner == 2 and outer == 4
    tok = P(("expert", "dp"), None)
    w = P("expert", "dp", None)
    return jax.shard_map(
        paired if lines else on_device, mesh=mesh, in_specs=(tok, tok, tok, tok, w, w),
        out_specs=(tok, tok, w), check_vma=False)
```

```python
import functools

import jax
import jax.numpy as jnp
from jax import lax
from jax.experimental import pallas as pl
from jax.experimental.pallas import tpu as pltpu
from jax.sharding import PartitionSpec as P

CAP = 12
PAD = 16
LANES = 128
FOLD = CAP // (PAD - CAP)
BF = jnp.bfloat16
F32 = jnp.float32


def dot(left, right, dims=((1,), (0,))):
    return lax.dot_general(left, right, (dims, ((), ())), preferred_element_type=F32)


def ring_kernel(groups, outer, inner, tok, dout, ids, scores, gate_in, down_in,
           o_tok, o_gates, o_down,
           gate_buf, down_buf, x_ch, up_ch, pre_acc, u_acc, send, recv, hid_buf, dx_send, dx_buf, ret, back,
           w_send, w_recv, own_sem, s_send, s_recv, h_send, h_recv, x_send, x_recv, b_send, b_recv):
    n = outer * inner
    me = lax.axis_index("dp")
    mine = lax.axis_index("expert")
    zo = me // inner
    xi = me - zo * inner
    slots = groups * PAD
    rows = gate_in.shape[1]
    feats = tok.shape[1]
    width = down_in.shape[2]
    ins = (down_in, gate_in)
    bufs = (down_buf, gate_buf)

    barrier = pltpu.get_barrier_semaphore()
    for k in range(1, n):
        pl.semaphore_signal(barrier, inc=1, device_id={"dp": lax.rem(me + k, n)},
                            device_id_type=pl.DeviceIdType.MESH)
    for k in range(1, groups):
        pl.semaphore_signal(barrier, inc=1, device_id={"expert": lax.rem(mine + k, groups)},
                            device_id_type=pl.DeviceIdType.MESH)
    pl.semaphore_wait(barrier, n - 1 + groups - 1)

    def remote(src, dst, ss, rs, **where):
        return pltpu.make_async_remote_copy(
            src_ref=src, dst_ref=dst, send_sem=ss, recv_sem=rs,
            device_id=where, device_id_type=pl.DeviceIdType.MESH)

    def target(way):
        return me + (inner, -inner, 1, -1)[way]

    def can(way):
        return (zo < outer - 1, zo > 0, xi < inner - 1, xi > 0)[way]

    def hop(w, s, way, own=False):
        src = ins[w].at[0] if own else bufs[w].at[s]
        return remote(src, bufs[w].at[s], w_send.at[w, way, s], w_recv.at[w, s], dp=target(way))

    started = []
    accs = (u_acc, pre_acc)
    chunks = (up_ch, x_ch)

    def forward(w, s, way, valid, own=False):
        ok = can(way) if valid is None else jnp.logical_and(can(way), valid)

        @pl.when(ok)
        def _():
            hop(w, s, way, own).start()
        started.append((ok, w, s, way, own))

    def arrive(w, s, valid):
        @pl.when(valid)
        def _():
            hop(w, s, 0).wait_recv()

    def add(w, s, valid):
        @pl.when(valid)
        def _():
            accs[w][...] += dot(chunks[w][s], bufs[w][s])

    def outer_shards(d):
        return ((0, me - d * inner, zo >= d), (1, me + d * inner, zo + d < outer))

    def outer_step(w, d):
        for way, s, valid in outer_shards(d):
            arrive(w, s, valid)
            for go in (way, 2, 3):
                forward(w, s, go, valid)

    def outer_add(w, d):
        for _, s, valid in outer_shards(d):
            add(w, s, valid)

    def inner_step(w, d):
        for di in range(1, inner):
            for sign in ((1,) if d == 0 else (-1, 1)):
                so = zo + sign * d
                good = jnp.logical_and(so >= 0, so < outer)
                for way, step in ((2, -di), (3, di)):
                    xs = xi + step
                    valid = jnp.logical_and(good, jnp.logical_and(xs >= 0, xs < inner))
                    s = so * inner + xs
                    arrive(w, s, valid)
                    if inner > 2:
                        forward(w, s, way, valid)
                    add(w, s, valid)

    own = [pltpu.make_async_copy(ins[w].at[0], bufs[w].at[me], own_sem.at[w]) for w in range(2)]
    for way in range(4):
        forward(1, me, way, None, own=True)
    for way in range(4):
        forward(0, me, way, None, own=True)
    for c in own:
        c.start()

    t_rows = tok.shape[0]
    topk = ids.shape[0]
    row = lax.broadcasted_iota(jnp.int32, (slots, t_rows), 0)
    row_e = row // PAD
    row_r = (row - row_e * PAD).astype(F32)
    idv = ids[...]
    scv = scores[...].astype(F32)
    live = jnp.zeros((slots, t_rows), F32)
    gcol = jnp.zeros((slots, t_rows), F32)
    hits = []
    for k in range(topk):
        hit = idv[k:k + 1, :] == row_e
        hits.append(hit)
        live = jnp.where(hit, 1.0, live)
        gcol = jnp.where(hit, scv[k:k + 1, :], gcol)
    upper = (lax.broadcasted_iota(jnp.int32, (t_rows, t_rows), 0)
             < lax.broadcasted_iota(jnp.int32, (t_rows, t_rows), 1))
    rank = dot(live.astype(BF), jnp.where(upper, 1.0, 0.0).astype(BF))
    pick_t = jnp.where(rank == row_r, live, 0.0)
    pick_b = pick_t.astype(BF)
    send[:, 2 * feats:] = jnp.broadcast_to(
        jnp.sum(pick_t * gcol, axis=1, keepdims=True), (slots, LANES)).astype(BF)
    send[:, :feats] = dot(pick_b, tok[...]).astype(BF)
    send[:, feats:2 * feats] = dot(pick_b, dout[...]).astype(BF)

    def block(e):
        return pl.ds(pl.multiple_of(e * PAD, PAD), PAD)

    def swap(src, dst, ss, rs, k):
        e = lax.rem(mine + k, groups)
        return remote(src.at[block(e), :], dst.at[block(mine), :], ss.at[k], rs.at[k], expert=e)

    for k in range(1, groups):
        swap(send, recv, s_send, s_recv, k).start()
    recv[block(mine), :] = send[block(mine), :]
    pick = jnp.transpose(pick_t).astype(BF)

    def peer(src, dst, ss, rs, k, sliced):
        d = lax.rem(me + k, n)
        return remote(src.at[d] if sliced else src.at[me], dst.at[me], ss.at[k], rs.at[k], dp=d)

    if outer > 1:
        outer_step(1, 1)
        outer_step(0, 1)

    packed = groups * CAP
    pr = lax.broadcasted_iota(jnp.int32, (packed, slots), 0)
    pc = lax.broadcasted_iota(jnp.int32, (packed, slots), 1)
    pack = jnp.where(pc == (pr // CAP) * PAD + pr % CAP, 1.0, 0.0).astype(BF)

    for k in range(1, groups):
        swap(send, recv, s_send, s_recv, k).wait_recv()
    gates = recv[:, 2 * feats:2 * feats + 1].astype(F32)
    upstream = recv[:, feats:2 * feats]
    dexp = dot(pack, (gates * upstream.astype(F32)).astype(BF)).astype(BF)
    for d in range(n):
        dx_send[d] = dexp[:, d * rows:(d + 1) * rows]
        x_ch[d] = recv[:, d * rows:(d + 1) * rows]
        up_ch[d] = recv[:, feats + d * rows:feats + (d + 1) * rows]
    for k in range(1, n):
        peer(dx_send, dx_buf, x_send, x_recv, k, True).start()
    dx_buf[me] = dx_send[me]
    pre_acc[...] = dot(x_ch[me], gate_in[0])
    u_acc[...] = dot(up_ch[me], down_in[0])

    for d in range(2, outer):
        outer_step(1, d)
        outer_step(0, d)
        outer_add(1, d - 1)
        outer_add(0, d - 1)
    for d in range(outer - 1):
        inner_step(1, d)
        inner_step(0, d)
    if outer > 1:
        outer_add(1, outer - 1)
        outer_add(0, outer - 1)
    inner_step(1, outer - 1)

    pre = pre_acc[...]
    a = pre[:, :width]
    b = pre[:, width:]
    sig = jax.nn.sigmoid(a)
    act = a * sig
    hidden = (act * b).astype(BF)
    hid_buf[me] = dot(pack, hidden).astype(BF)
    for k in range(1, n):
        peer(hid_buf, hid_buf, h_send, h_recv, k, False).start()

    inner_step(0, outer - 1)
    for c in own:
        c.wait()

    u = u_acc[...]
    d_hid = gates * u
    d_pre = jnp.concatenate(
        [d_hid * b * sig * (1.0 + a * (1.0 - sig)), d_hid * act], axis=1).astype(BF)
    gate_full = gate_buf[...].reshape(n * rows, 2 * width)
    ret[:, feats:] = jnp.broadcast_to(
        jnp.sum(hidden.astype(F32) * u, axis=1, keepdims=True), (slots, LANES)).astype(BF)
    ret[:, :feats] = dot(d_pre, gate_full, ((1,), (1,))).astype(BF)
    for k in range(1, groups):
        swap(ret, back, b_send, b_recv, k).start()
    back[block(mine), :] = ret[block(mine), :]

    o_down[0] = dot(dx_buf[me], hid_buf[me], ((0,), (0,)))
    for k in range(1, n):
        s = lax.rem(me - k + n, n)
        peer(dx_send, dx_buf, x_send, x_recv, k, True).wait_recv()
        peer(hid_buf, hid_buf, h_send, h_recv, k, False).wait_recv()
        o_down[0] += dot(dx_buf[s], hid_buf[s], ((0,), (0,)))

    for k in range(1, groups):
        swap(ret, back, b_send, b_recv, k).wait_recv()
    o_tok[...] = dot(pick, back[:, :feats]).astype(BF)
    weighted = pick_t * back[:, feats:feats + 1].astype(F32)
    o_gates[...] = jnp.concatenate(
        [jnp.sum(jnp.where(hit, weighted, 0.0), axis=0, keepdims=True) for hit in hits],
        axis=0).astype(BF)

    for ok, w, s, way, is_own in started:
        @pl.when(ok)
        def _(w=w, s=s, way=way, is_own=is_own):
            hop(w, s, way, is_own).wait_send()
    for k in range(1, groups):
        swap(send, recv, s_send, s_recv, k).wait_send()
        swap(ret, back, b_send, b_recv, k).wait_send()
    for k in range(1, n):
        peer(dx_send, dx_buf, x_send, x_recv, k, True).wait_send()
        peer(hid_buf, hid_buf, h_send, h_recv, k, False).wait_send()

def remote(src, dst, ss, rs, **where):
    return pltpu.make_async_remote_copy(
        src_ref=src, dst_ref=dst, send_sem=ss, recv_sem=rs,
        device_id=where, device_id_type=pl.DeviceIdType.MESH)


def spread(blocks, j, down):
    size = blocks * PAD
    r = lax.broadcasted_iota(jnp.int32, (size, size), 0)
    c = lax.broadcasted_iota(jnp.int32, (size, size), 1)
    if not down:
        r, c = c, r
    i = r % PAD - CAP
    hit = jnp.logical_and(jnp.logical_and(r // PAD == c // PAD, i >= 0), c % PAD == FOLD * i + j)
    return jnp.where(hit, 1.0, 0.0).astype(BF)


def mid_kernel(groups, gate_in, down_in, tok_in, dout_in, ids_in, sc_in,
               o_tok, o_gates, o_down,
               gate_buf, down_buf, tok_v, dout_v, ids_v, sc_v, x_out, d_out, x_in, d_in, pre_acc, v_acc,
               dx_send, dx_buf, hid_buf, ret_a, ret_b, back_a, back_b, pack_v, spread_v,
               l_sem, w_send, w_recv, s_send, s_recv, x_send, x_recv,
               h_send, h_recv, b_send, b_recv):
    me = lax.axis_index("dp")
    mine = lax.axis_index("expert")
    zo = me // 2
    xi = me - 2 * zo
    side = zo // 2
    mid = jnp.logical_or(zo == 1, zo == 2)
    end = jnp.logical_not(mid)
    slots = groups * PAD
    rows = gate_in.shape[1]
    feats = tok_in.shape[1]
    width = down_in.shape[2]
    n = feats // rows

    def at(x, z):
        return 2 * z + x

    xo = 1 - xi
    pal = at(xo, zo)
    z_mid, z_end, z_far, z_edge = 1 + side, 3 * side, 2 - side, 3 - 3 * side
    my_mid, my_end = at(xi, z_mid), at(xi, z_end)
    far_mid, far_end = at(xi, z_far), at(xi, z_edge)
    line = jnp.where(mid, far_mid, my_mid)

    barrier = pltpu.get_barrier_semaphore()

    def greet(**where):
        pl.semaphore_signal(barrier, inc=1, device_id=where, device_id_type=pl.DeviceIdType.MESH)

    greet(dp=pal)

    @pl.when(mid)
    def _():
        greet(dp=far_mid)
        for e in range(groups):
            greet(dp=my_end, expert=e)
        for k in range(1, groups):
            greet(expert=lax.rem(mine + k, groups))

    local = [pltpu.make_async_copy(src, dst, l_sem.at[i]) for i, (src, dst) in enumerate((
        (gate_in.at[0], gate_buf.at[me]), (down_in.at[0], down_buf.at[me]),
        (ids_in, ids_v), (sc_in, sc_v), (tok_in, tok_v), (dout_in, dout_v)))]
    for c in local:
        c.start()
    pl.semaphore_wait(barrier, 1 + groups)

    def piece(s, p, way, own=False):
        if p < 4:
            part = pl.ds(p * (rows // 4), rows // 4)
            src = gate_buf.at[s, part]
            dst = gate_buf.at[s, part]
        else:
            part = pl.ds((p - 4) * (rows // 2), rows // 2)
            src = down_buf.at[s, part]
            dst = down_buf.at[s, part]
        return remote(src, dst, w_send.at[way, s, p], w_recv.at[s, p], dp=(line, pal)[way])

    def own_out(way, *ps):
        for p in ps:
            piece(me, p, way, True).start()

    def take(s, p, *out):
        piece(s, p, 0).wait_recv()
        for way in out:
            piece(s, p, way).start()

    for c in local[:2]:
        c.wait()
    for p in range(4):
        own_out(0, p)
        own_out(1, p)

    @pl.when(end)
    def _():
        for p in (4, 5):
            own_out(0, p)
            own_out(1, p)

    for c in local[2:]:
        c.wait()
    t_rows = tok_v.shape[0]
    topk = ids_v.shape[0]
    row = lax.broadcasted_iota(jnp.int32, (slots, t_rows), 0)
    row_e = row // PAD
    row_r = (row - row_e * PAD).astype(F32)
    idv = ids_v[...]
    scv = sc_v[...].astype(F32)
    live = jnp.zeros((slots, t_rows), F32)
    gcol = jnp.zeros((slots, t_rows), F32)
    hits = []
    for k in range(topk):
        hit = idv[k:k + 1, :] == row_e
        hits.append(hit)
        live = jnp.where(hit, 1.0, live)
        gcol = jnp.where(hit, scv[k:k + 1, :], gcol)
    upper = (lax.broadcasted_iota(jnp.int32, (t_rows, t_rows), 0)
             < lax.broadcasted_iota(jnp.int32, (t_rows, t_rows), 1))
    rank = dot(live.astype(BF), jnp.where(upper, 1.0, 0.0).astype(BF))
    pick_t = jnp.where(rank == row_r, live, 0.0)
    pick_b = pick_t.astype(BF)
    gate_col = jnp.sum(pick_t * gcol, axis=1, keepdims=True)

    def block(i):
        start = i * PAD
        return pl.ds(start if isinstance(i, int) else pl.multiple_of(start, PAD), PAD)

    outs, ins = (x_out, d_out), (x_in, d_in)
    quarter = feats // 4
    sent_cols = (pl.ds(0, 3 * quarter), pl.ds(0, LANES + 3 * quarter))

    def fold_in(kind, whole):
        base = kind * LANES
        behind = whole[:, 3 * quarter:]
        for j in range(FOLD):
            part = whole[:, j * quarter:(j + 1) * quarter].astype(F32) + dot(spread(groups, j, True), behind)
            outs[kind][:, base + j * quarter:base + (j + 1) * quarter] = part.astype(BF)

    def unfold(kind):
        base = kind * LANES
        tail = sum(dot(spread(2 * groups, j, False), ins[kind][:, base + j * quarter:base + (j + 1) * quarter])
                   for j in range(FOLD))
        ins[kind][:, base + 3 * quarter:base + feats] = tail.astype(BF)

    def slots_to(kind, e, place):
        return remote(outs[kind].at[block(e), :], ins[kind].at[block(place * groups + mine), sent_cols[kind]],
                      s_send.at[kind, e], s_recv.at[kind, place, mine], dp=my_mid, expert=e)

    def slots_from(kind, place, e):
        return remote(outs[kind].at[block(e), :], ins[kind].at[block(place * groups + e), sent_cols[kind]],
                      s_send.at[kind, e], s_recv.at[kind, place, e], dp=my_mid, expert=e)

    def other(k):
        return lax.rem(mine + k, groups)

    def slots_out(kind):
        @pl.when(end)
        def _():
            for e in range(groups):
                slots_to(kind, e, 1).start()

        @pl.when(mid)
        def _():
            for k in range(1, groups):
                slots_to(kind, other(k), 0).start()
            ins[kind][block(mine), sent_cols[kind]] = outs[kind][block(mine), :]

    fold_in(0, dot(pick_b, tok_v[...]).astype(BF))
    slots_out(0)
    d_out[:, :LANES] = jnp.broadcast_to(gate_col, (slots, LANES)).astype(BF)
    fold_in(1, (gate_col * dot(pick_b, dout_v[...])).astype(BF))

    @pl.when(end)
    def _():
        for p in range(4):
            take(pal, p, 0)

    slots_out(1)

    @pl.when(end)
    def _():
        for p in (4, 5):
            take(pal, p, 0)

    pick = jnp.transpose(pick_t).astype(BF)
    folded = [dot(pick, spread(groups, j, False)).astype(BF) for j in range(FOLD)]

    def dx_to(d):
        return remote(dx_send.at[d], dx_buf.at[2 * side + xi], x_send.at[d], x_recv.at[2 * side + xi], dp=d)

    def dx_from(q):
        return remote(dx_send.at[0], dx_buf.at[q], x_send.at[0], x_recv.at[q], dp=pal)

    def hid(q, d):
        return remote(hid_buf.at[q], hid_buf.at[q], h_send.at[q, d], h_recv.at[q], dp=d)

    rets, backs = (ret_a, ret_b), (back_a, back_b)

    def ret_to(part, place, e):
        return remote(rets[part].at[block(place * groups + e), :], backs[part].at[block(mine), :],
                      b_send.at[part, place, e], b_recv.at[part, mine], dp=(my_mid, my_end)[place], expert=e)

    def back_from(part, e):
        return remote(rets[part].at[block(e), :], backs[part].at[block(e), :],
                      b_send.at[part, 0, e], b_recv.at[part, e], dp=my_mid, expert=e)

    def ret_out(part):
        for e in range(groups):
            ret_to(part, 1, e).start()
        for k in range(1, groups):
            ret_to(part, 0, other(k)).start()
        backs[part][block(mine), :] = rets[part][block(mine), :]

    my_q, pal_q = 2 * side + xi, 2 * side + xo
    far_q, fpal_q = 2 - 2 * side + xi, 2 - 2 * side + xo
    a, b, c, d, e_, f, g = (my_end, at(xo, z_end), pal, far_mid, far_end, at(xo, z_far), at(xo, z_edge))

    @pl.when(mid)
    def _():
        many = 2 * slots
        packed = 2 * groups * CAP

        def cols(s, base=0):
            return pl.ds(pl.multiple_of(base + s * rows, LANES), rows)

        def add(s):
            pre_acc[...] += dot(x_in[:, cols(s)], gate_buf[s])

        def add_v(s):
            v_acc[...] += dot(d_in[:, cols(s, LANES)], down_buf[s])

        def slots_wait(kind):
            for k in range(1, groups):
                slots_from(kind, 0, other(k)).wait_recv()
            for e in range(groups):
                slots_from(kind, 1, e).wait_recv()
            unfold(kind)

        pr = lax.broadcasted_iota(jnp.int32, (packed, many), 0)
        pc = lax.broadcasted_iota(jnp.int32, (packed, many), 1)
        pack_v[...] = jnp.where(pc == (pr // CAP) * PAD + pr % CAP, 1.0, 0.0).astype(BF)
        for j in range(FOLD):
            spread_v[j] = spread(2 * groups, j, True)
        take(a, 0, 0)
        take(a, 1, 0)
        take(d, 2, 1)
        own_out(1, 4)
        take(a, 2, 0)
        take(d, 3, 1)
        take(a, 3, 0)
        take(c, 0, 0)
        take(c, 1, 0)
        own_out(0, 4, 5)
        take(a, 4, 0)
        take(a, 5, 0)
        for p in range(4):
            take(e_, p, 1)
        own_out(1, 5)
        slots_wait(0)
        pre_acc[...] = dot(x_in[:, cols(me)], gate_buf[me])
        take(c, 2)
        take(c, 3)
        take(d, 0)
        take(d, 1)
        for s in (a, c, d, e_):
            add(s)
        def rest(s):
            for p in range(4):
                take(s, p)
            add(s)

        rest(f)
        rest(g)
        rest(b)

        pre = pre_acc[...]
        ga = pre[:, :width]
        gb = pre[:, width:]
        sig = jax.nn.sigmoid(ga)
        act = ga * sig
        slope = gb * sig * (1.0 + ga * (1.0 - sig))
        hidden = (act * gb).astype(BF)
        hid_buf[my_q] = dot(pack_v[...], hidden).astype(BF)
        hid(my_q, my_end).start()
        hid(my_q, far_end).start()
        take(c, 4, 0)
        take(d, 5, 1)
        take(e_, 4, 1)
        take(e_, 5, 1)
        for s in (pal, far_mid):
            hid(my_q, s).start()

        slots_wait(1)
        dexp = dot(pack_v[...], d_in[:, LANES:]).astype(BF)
        for s in range(n):
            dx_send[s] = dexp[:, s * rows:(s + 1) * rows]
        for s in (e_, g, a, b, d, f, c):
            dx_to(s).start()
        dx_buf[my_q] = dx_send[me]
        gates = d_in[:, :1].astype(F32)
        inverse = jnp.where(gates > 0.0, 1.0 / jnp.where(gates > 0.0, gates, 1.0), 0.0)
        v_acc[...] = dot(d_in[:, cols(me, LANES)], down_buf[me])
        take(c, 5)
        take(d, 4)
        for s in (a, c, d, e_):
            add_v(s)
        for s in (f, b, g):
            take(s, 4)
            take(s, 5)
            add_v(s)

        used = lax.broadcasted_iota(jnp.int32, (many, width), 0) % PAD < CAP
        d_hid = jnp.where(used, v_acc[...], 0.0)
        d_pre = jnp.concatenate([d_hid * slope, d_hid * act], axis=1).astype(BF)
        quarter = feats // 4

        def d_slot(j):
            w = gate_buf[j * n // 4:(j + 1) * n // 4].reshape(quarter, 2 * width)
            return dot(d_pre, w, ((1,), (1,)))

        last = d_slot(3).astype(BF)

        def fold(j):
            return (d_slot(j) + dot(spread_v[j], last)).astype(BF)

        ret_a[...] = fold(0)
        ret_out(0)
        for j in range(1, FOLD):
            ret_b[:, (j - 1) * quarter:j * quarter] = fold(j)
        slot_grad = jnp.sum(hidden.astype(F32) * d_hid, axis=1, keepdims=True) * inverse
        ret_b[:, 2 * quarter:] = jnp.broadcast_to(slot_grad, (many, LANES)).astype(BF)
        ret_out(1)

        hid(far_q, me).wait_recv()
        hid(far_q, pal).start()
        o_down[0] = dot(dx_buf[my_q], hid_buf[my_q], ((0,), (0,)))
        dx_from(far_q).wait_recv()
        o_down[0] += dot(dx_buf[far_q], hid_buf[far_q], ((0,), (0,)))

    @pl.when(end)
    def _():
        for q in (my_q, far_q):
            hid(q, me).wait_recv()
            hid(q, pal).start()
        dx_from(my_q).wait_recv()
        dx_from(far_q).wait_recv()
        o_down[0] = (dot(dx_buf[my_q], hid_buf[my_q], ((0,), (0,)))
                     + dot(dx_buf[far_q], hid_buf[far_q], ((0,), (0,))))

    def grow(q):
        hid(q, me).wait_recv()
        dx_from(q).wait_recv()
        o_down[0] += dot(dx_buf[q], hid_buf[q], ((0,), (0,)))

    grow(pal_q)
    quarter = feats // 4

    def back_wait(part):
        for k in range(1, groups):
            back_from(part, other(k)).wait_recv()
        pl.when(end)(lambda: back_from(part, mine).wait_recv())

    back_wait(0)
    o_tok[:, :quarter] = dot(pick, back_a[...]).astype(BF)
    last = dot(folded[0], back_a[...])
    grow(fpal_q)
    back_wait(1)
    for j in range(1, FOLD):
        part = back_b[:, (j - 1) * quarter:j * quarter]
        o_tok[:, j * quarter:(j + 1) * quarter] = dot(pick, part).astype(BF)
        last += dot(folded[j], part)
    o_tok[:, 3 * quarter:] = last.astype(BF)
    weighted = pick_t * back_b[:, 2 * quarter:2 * quarter + 1].astype(F32)
    o_gates[...] = jnp.concatenate(
        [jnp.sum(jnp.where(hit, weighted, 0.0), axis=0, keepdims=True) for hit in hits],
        axis=0).astype(BF)

    for p in range(6):
        for way in range(2):
            piece(me, p, way, True).wait_send()

    @pl.when(end)
    def _():
        for e in range(groups):
            slots_to(0, e, 1).wait_send()
            slots_to(1, e, 1).wait_send()
        for p in range(6):
            piece(pal, p, 0).wait_send()
        for q in (my_q, far_q):
            hid(q, pal).wait_send()

    @pl.when(mid)
    def _():
        for p in range(6):
            piece(a, p, 0).wait_send()
        for s, p, way in ((c, 0, 0), (c, 1, 0), (c, 4, 0), (d, 2, 1), (d, 3, 1), (d, 5, 1)):
            piece(s, p, way).wait_send()
        for p in range(6):
            piece(e_, p, 1).wait_send()
        for k in range(1, groups):
            slots_to(0, other(k), 0).wait_send()
            slots_to(1, other(k), 0).wait_send()
            for part in range(2):
                ret_to(part, 0, other(k)).wait_send()
        for e in range(groups):
            for part in range(2):
                ret_to(part, 1, e).wait_send()
        for s in (far_end, far_mid, my_end, pal):
            hid(my_q, s).wait_send()
        hid(far_q, pal).wait_send()
        for s in (a, b, c, d, e_, f, g):
            dx_to(s).wait_send()


def place(*refs):
    ins, outs, sem = refs[:3], refs[3:6], refs[6]
    copies = [pltpu.make_async_copy(src, dst, sem.at[i]) for i, (src, dst) in enumerate(zip(ins, outs))]
    for c in copies:
        c.start()
    for c in copies:
        c.wait()


def place_whole(*refs):
    for src, dst in zip(refs[:3], refs[3:]):
        dst[...] = src[...]


def solution(mesh):
    groups = mesh.shape["expert"]
    n = mesh.shape["dp"]
    inner = 1
    while n % (inner * 2) == 0 and (inner * 2) ** 2 <= n:
        inner *= 2
    outer = n // inner

    def on_device(tokens, d_output, expert_ids, gate_scores, gate_up_w, down_w):
        feats = tokens.shape[1]
        rows = gate_up_w.shape[1]
        width = down_w.shape[2]
        slots = groups * PAD
        packed = groups * CAP
        vmem = pl.BlockSpec(memory_space=pltpu.VMEM)
        dma = pltpu.SemaphoreType.DMA
        grads, d_gates, d_down = pl.pallas_call(
            functools.partial(ring_kernel, groups, outer, inner),
            out_shape=(
                jax.ShapeDtypeStruct(tokens.shape, BF),
                jax.ShapeDtypeStruct(gate_scores.shape[::-1], BF),
                jax.ShapeDtypeStruct(down_w.shape, F32),
            ),
            in_specs=[vmem] * 6,
            out_specs=(vmem,) * 3,
            scratch_shapes=[
                pltpu.VMEM((n, rows, 2 * width), BF),
                pltpu.VMEM((n, rows, width), BF),
                pltpu.VMEM((n, slots, rows), BF),
                pltpu.VMEM((n, slots, rows), BF),
                pltpu.VMEM((slots, 2 * width), F32),
                pltpu.VMEM((slots, width), F32),
                pltpu.VMEM((slots, 2 * feats + LANES), BF),
                pltpu.VMEM((slots, 2 * feats + LANES), BF),
                pltpu.VMEM((n, packed, width), BF),
                pltpu.VMEM((n, packed, rows), BF),
                pltpu.VMEM((n, packed, rows), BF),
                pltpu.VMEM((slots, feats + LANES), BF),
                pltpu.VMEM((slots, feats + LANES), BF),
                dma((2, 4, n)), dma((2, n)), dma((2,)),
                dma((groups,)), dma((groups,)),
                dma((n,)), dma((n,)),
                dma((n,)), dma((n,)),
                dma((groups,)), dma((groups,)),
            ],
            compiler_params=pltpu.CompilerParams(
                collective_id=0, has_side_effects=True, vmem_limit_bytes=60 * 2**20),
        )(tokens, d_output, expert_ids.T, gate_scores.T, gate_up_w, down_w)
        grads, d_gates, d_down = pl.pallas_call(
            place_whole,
            out_shape=tuple(jax.ShapeDtypeStruct(v.shape, v.dtype) for v in (grads, d_gates, d_down)),
            in_specs=[vmem] * 3,
            out_specs=(vmem,) * 3,
        )(grads, d_gates, d_down)
        return grads, d_gates.T, d_down

    def paired(tokens, d_output, expert_ids, gate_scores, gate_up_w, down_w):
        t_rows, feats = tokens.shape
        topk = expert_ids.shape[1]
        rows = gate_up_w.shape[1]
        width = down_w.shape[2]
        slots = groups * PAD
        packed = 2 * groups * CAP
        vmem = pl.BlockSpec(memory_space=pltpu.VMEM)
        hbm = pl.BlockSpec(memory_space=pltpu.HBM)
        dma = pltpu.SemaphoreType.DMA
        shapes = (
            jax.ShapeDtypeStruct(tokens.shape, BF),
            jax.ShapeDtypeStruct(gate_scores.shape[::-1], BF),
            jax.ShapeDtypeStruct(down_w.shape, F32),
        )
        parts = pl.pallas_call(
            functools.partial(mid_kernel, groups),
            out_shape=shapes,
            in_specs=[hbm] * 6,
            out_specs=(vmem,) * 3,
            scratch_shapes=[
                pltpu.VMEM((n, rows, 2 * width), BF),
                pltpu.VMEM((n, rows, width), BF),
                pltpu.VMEM((t_rows, feats), BF),
                pltpu.VMEM((t_rows, feats), BF),
                pltpu.VMEM((topk, t_rows), jnp.int32),
                pltpu.VMEM((topk, t_rows), BF),
                pltpu.VMEM((slots, feats // 4 * 3), BF),
                pltpu.VMEM((slots, feats // 4 * 3 + LANES), BF),
                pltpu.VMEM((2 * slots, feats), BF),
                pltpu.VMEM((2 * slots, feats + LANES), BF),
                pltpu.VMEM((2 * slots, 2 * width), F32),
                pltpu.VMEM((2 * slots, width), F32),
                pltpu.VMEM((n, packed, rows), BF),
                pltpu.VMEM((4, packed, rows), BF),
                pltpu.VMEM((4, packed, width), BF),
                pltpu.VMEM((2 * slots, feats // 4), BF),
                pltpu.VMEM((2 * slots, feats // 2 + LANES), BF),
                pltpu.VMEM((slots, feats // 4), BF),
                pltpu.VMEM((slots, feats // 2 + LANES), BF),
                pltpu.VMEM((packed, 2 * slots), BF),
                pltpu.VMEM((FOLD, 2 * slots, 2 * slots), BF),
                dma((6,)),
                dma((2, n, 6)), dma((n, 6)),
                dma((2, groups)), dma((2, 2, groups)),
                dma((n,)), dma((4,)),
                dma((4, n)), dma((4,)),
                dma((2, 2, groups)), dma((2, groups)),
            ],
            compiler_params=pltpu.CompilerParams(
                collective_id=0, has_side_effects=True, vmem_limit_bytes=16 * 2**20),
        )(*(pltpu.with_memory_space_constraint(v, pltpu.HBM) for v in (
            gate_up_w, down_w, tokens, d_output, expert_ids.T, gate_scores.T)))
        grads, d_gates, d_down = pl.pallas_call(
            place,
            out_shape=shapes,
            in_specs=[vmem] * 3,
            out_specs=(hbm,) * 3,
            scratch_shapes=[dma((3,))],
            compiler_params=pltpu.CompilerParams(vmem_limit_bytes=2**20),
        )(*parts)
        return grads, d_gates.T, d_down

    lines = inner == 2 and outer == 4
    tok = P(("expert", "dp"), None)
    w = P("expert", "dp", None)
    return jax.shard_map(
        paired if lines else on_device, mesh=mesh, in_specs=(tok, tok, tok, tok, w, w),
        out_specs=(tok, tok, w), check_vma=False)
```

```python
import functools

import jax
import jax.numpy as jnp
from jax import lax
from jax.experimental import pallas as pl
from jax.experimental.pallas import tpu as pltpu
from jax.sharding import PartitionSpec as P

CAP = 12
PAD = 16
LANES = 128
FOLD = CAP // (PAD - CAP)
BF = jnp.bfloat16
F32 = jnp.float32


def dot(left, right, dims=((1,), (0,))):
    return lax.dot_general(left, right, (dims, ((), ())), preferred_element_type=F32)


def ring_kernel(groups, outer, inner, tok, dout, ids, scores, gate_in, down_in,
           o_tok, o_gates, o_down,
           gate_buf, down_buf, x_ch, up_ch, pre_acc, u_acc, send, recv, hid_buf, dx_send, dx_buf, ret, back,
           w_send, w_recv, own_sem, s_send, s_recv, h_send, h_recv, x_send, x_recv, b_send, b_recv):
    n = outer * inner
    me = lax.axis_index("dp")
    mine = lax.axis_index("expert")
    zo = me // inner
    xi = me - zo * inner
    slots = groups * PAD
    rows = gate_in.shape[1]
    feats = tok.shape[1]
    width = down_in.shape[2]
    ins = (down_in, gate_in)
    bufs = (down_buf, gate_buf)

    barrier = pltpu.get_barrier_semaphore()
    for k in range(1, n):
        pl.semaphore_signal(barrier, inc=1, device_id={"dp": lax.rem(me + k, n)},
                            device_id_type=pl.DeviceIdType.MESH)
    for k in range(1, groups):
        pl.semaphore_signal(barrier, inc=1, device_id={"expert": lax.rem(mine + k, groups)},
                            device_id_type=pl.DeviceIdType.MESH)
    pl.semaphore_wait(barrier, n - 1 + groups - 1)

    def remote(src, dst, ss, rs, **where):
        return pltpu.make_async_remote_copy(
            src_ref=src, dst_ref=dst, send_sem=ss, recv_sem=rs,
            device_id=where, device_id_type=pl.DeviceIdType.MESH)

    def target(way):
        return me + (inner, -inner, 1, -1)[way]

    def can(way):
        return (zo < outer - 1, zo > 0, xi < inner - 1, xi > 0)[way]

    def hop(w, s, way, own=False):
        src = ins[w].at[0] if own else bufs[w].at[s]
        return remote(src, bufs[w].at[s], w_send.at[w, way, s], w_recv.at[w, s], dp=target(way))

    started = []
    accs = (u_acc, pre_acc)
    chunks = (up_ch, x_ch)

    def forward(w, s, way, valid, own=False):
        ok = can(way) if valid is None else jnp.logical_and(can(way), valid)

        @pl.when(ok)
        def _():
            hop(w, s, way, own).start()
        started.append((ok, w, s, way, own))

    def arrive(w, s, valid):
        @pl.when(valid)
        def _():
            hop(w, s, 0).wait_recv()

    def add(w, s, valid):
        @pl.when(valid)
        def _():
            accs[w][...] += dot(chunks[w][s], bufs[w][s])

    def outer_shards(d):
        return ((0, me - d * inner, zo >= d), (1, me + d * inner, zo + d < outer))

    def outer_step(w, d):
        for way, s, valid in outer_shards(d):
            arrive(w, s, valid)
            for go in (way, 2, 3):
                forward(w, s, go, valid)

    def outer_add(w, d):
        for _, s, valid in outer_shards(d):
            add(w, s, valid)

    def inner_step(w, d):
        for di in range(1, inner):
            for sign in ((1,) if d == 0 else (-1, 1)):
                so = zo + sign * d
                good = jnp.logical_and(so >= 0, so < outer)
                for way, step in ((2, -di), (3, di)):
                    xs = xi + step
                    valid = jnp.logical_and(good, jnp.logical_and(xs >= 0, xs < inner))
                    s = so * inner + xs
                    arrive(w, s, valid)
                    if inner > 2:
                        forward(w, s, way, valid)
                    add(w, s, valid)

    own = [pltpu.make_async_copy(ins[w].at[0], bufs[w].at[me], own_sem.at[w]) for w in range(2)]
    for way in range(4):
        forward(1, me, way, None, own=True)
    for way in range(4):
        forward(0, me, way, None, own=True)
    for c in own:
        c.start()

    t_rows = tok.shape[0]
    topk = ids.shape[0]
    row = lax.broadcasted_iota(jnp.int32, (slots, t_rows), 0)
    row_e = row // PAD
    row_r = (row - row_e * PAD).astype(F32)
    idv = ids[...]
    scv = scores[...].astype(F32)
    live = jnp.zeros((slots, t_rows), F32)
    gcol = jnp.zeros((slots, t_rows), F32)
    hits = []
    for k in range(topk):
        hit = idv[k:k + 1, :] == row_e
        hits.append(hit)
        live = jnp.where(hit, 1.0, live)
        gcol = jnp.where(hit, scv[k:k + 1, :], gcol)
    upper = (lax.broadcasted_iota(jnp.int32, (t_rows, t_rows), 0)
             < lax.broadcasted_iota(jnp.int32, (t_rows, t_rows), 1))
    rank = dot(live.astype(BF), jnp.where(upper, 1.0, 0.0).astype(BF))
    pick_t = jnp.where(rank == row_r, live, 0.0)
    pick_b = pick_t.astype(BF)
    send[:, 2 * feats:] = jnp.broadcast_to(
        jnp.sum(pick_t * gcol, axis=1, keepdims=True), (slots, LANES)).astype(BF)
    send[:, :feats] = dot(pick_b, tok[...]).astype(BF)
    send[:, feats:2 * feats] = dot(pick_b, dout[...]).astype(BF)

    def block(e):
        return pl.ds(pl.multiple_of(e * PAD, PAD), PAD)

    def swap(src, dst, ss, rs, k):
        e = lax.rem(mine + k, groups)
        return remote(src.at[block(e), :], dst.at[block(mine), :], ss.at[k], rs.at[k], expert=e)

    for k in range(1, groups):
        swap(send, recv, s_send, s_recv, k).start()
    recv[block(mine), :] = send[block(mine), :]
    pick = jnp.transpose(pick_t).astype(BF)

    def peer(src, dst, ss, rs, k, sliced):
        d = lax.rem(me + k, n)
        return remote(src.at[d] if sliced else src.at[me], dst.at[me], ss.at[k], rs.at[k], dp=d)

    if outer > 1:
        outer_step(1, 1)
        outer_step(0, 1)

    packed = groups * CAP
    pr = lax.broadcasted_iota(jnp.int32, (packed, slots), 0)
    pc = lax.broadcasted_iota(jnp.int32, (packed, slots), 1)
    pack = jnp.where(pc == (pr // CAP) * PAD + pr % CAP, 1.0, 0.0).astype(BF)

    for k in range(1, groups):
        swap(send, recv, s_send, s_recv, k).wait_recv()
    gates = recv[:, 2 * feats:2 * feats + 1].astype(F32)
    upstream = recv[:, feats:2 * feats]
    dexp = dot(pack, (gates * upstream.astype(F32)).astype(BF)).astype(BF)
    for d in range(n):
        dx_send[d] = dexp[:, d * rows:(d + 1) * rows]
        x_ch[d] = recv[:, d * rows:(d + 1) * rows]
        up_ch[d] = recv[:, feats + d * rows:feats + (d + 1) * rows]
    for k in range(1, n):
        peer(dx_send, dx_buf, x_send, x_recv, k, True).start()
    dx_buf[me] = dx_send[me]
    pre_acc[...] = dot(x_ch[me], gate_in[0])
    u_acc[...] = dot(up_ch[me], down_in[0])

    for d in range(2, outer):
        outer_step(1, d)
        outer_step(0, d)
        outer_add(1, d - 1)
        outer_add(0, d - 1)
    for d in range(outer - 1):
        inner_step(1, d)
        inner_step(0, d)
    if outer > 1:
        outer_add(1, outer - 1)
        outer_add(0, outer - 1)
    inner_step(1, outer - 1)

    pre = pre_acc[...]
    a = pre[:, :width]
    b = pre[:, width:]
    sig = jax.nn.sigmoid(a)
    act = a * sig
    hidden = (act * b).astype(BF)
    hid_buf[me] = dot(pack, hidden).astype(BF)
    for k in range(1, n):
        peer(hid_buf, hid_buf, h_send, h_recv, k, False).start()

    inner_step(0, outer - 1)
    for c in own:
        c.wait()

    u = u_acc[...]
    d_hid = gates * u
    d_pre = jnp.concatenate(
        [d_hid * b * sig * (1.0 + a * (1.0 - sig)), d_hid * act], axis=1).astype(BF)
    gate_full = gate_buf[...].reshape(n * rows, 2 * width)
    ret[:, feats:] = jnp.broadcast_to(
        jnp.sum(hidden.astype(F32) * u, axis=1, keepdims=True), (slots, LANES)).astype(BF)
    ret[:, :feats] = dot(d_pre, gate_full, ((1,), (1,))).astype(BF)
    for k in range(1, groups):
        swap(ret, back, b_send, b_recv, k).start()
    back[block(mine), :] = ret[block(mine), :]

    o_down[0] = dot(dx_buf[me], hid_buf[me], ((0,), (0,)))
    for k in range(1, n):
        s = lax.rem(me - k + n, n)
        peer(dx_send, dx_buf, x_send, x_recv, k, True).wait_recv()
        peer(hid_buf, hid_buf, h_send, h_recv, k, False).wait_recv()
        o_down[0] += dot(dx_buf[s], hid_buf[s], ((0,), (0,)))

    for k in range(1, groups):
        swap(ret, back, b_send, b_recv, k).wait_recv()
    o_tok[...] = dot(pick, back[:, :feats]).astype(BF)
    weighted = pick_t * back[:, feats:feats + 1].astype(F32)
    o_gates[...] = jnp.concatenate(
        [jnp.sum(jnp.where(hit, weighted, 0.0), axis=0, keepdims=True) for hit in hits],
        axis=0).astype(BF)

    for ok, w, s, way, is_own in started:
        @pl.when(ok)
        def _(w=w, s=s, way=way, is_own=is_own):
            hop(w, s, way, is_own).wait_send()
    for k in range(1, groups):
        swap(send, recv, s_send, s_recv, k).wait_send()
        swap(ret, back, b_send, b_recv, k).wait_send()
    for k in range(1, n):
        peer(dx_send, dx_buf, x_send, x_recv, k, True).wait_send()
        peer(hid_buf, hid_buf, h_send, h_recv, k, False).wait_send()

def remote(src, dst, ss, rs, **where):
    return pltpu.make_async_remote_copy(
        src_ref=src, dst_ref=dst, send_sem=ss, recv_sem=rs,
        device_id=where, device_id_type=pl.DeviceIdType.MESH)


def spread(blocks, j, down):
    size = blocks * PAD
    r = lax.broadcasted_iota(jnp.int32, (size, size), 0)
    c = lax.broadcasted_iota(jnp.int32, (size, size), 1)
    if not down:
        r, c = c, r
    i = r % PAD - CAP
    hit = jnp.logical_and(jnp.logical_and(r // PAD == c // PAD, i >= 0), c % PAD == FOLD * i + j)
    return jnp.where(hit, 1.0, 0.0).astype(BF)


def mid_kernel(groups, gate_in, down_in, tok_in, dout_in, ids_in, sc_in,
               o_tok, o_gates, o_down,
               gate_buf, down_buf, tok_v, dout_v, ids_v, sc_v, x_out, d_out, x_in, d_in, pre_acc, v_acc,
               dx_send, dx_buf, hid_buf, ret_a, ret_b, back_a, back_b, pack_v, spread_v,
               l_sem, w_send, w_recv, s_send, s_recv, x_send, x_recv,
               h_send, h_recv, b_send, b_recv):
    me = lax.axis_index("dp")
    mine = lax.axis_index("expert")
    zo = me // 2
    xi = me - 2 * zo
    side = zo // 2
    mid = jnp.logical_or(zo == 1, zo == 2)
    end = jnp.logical_not(mid)
    slots = groups * PAD
    rows = gate_in.shape[1]
    feats = tok_in.shape[1]
    width = down_in.shape[2]
    n = feats // rows

    def at(x, z):
        return 2 * z + x

    xo = 1 - xi
    pal = at(xo, zo)
    z_mid, z_end, z_far, z_edge = 1 + side, 3 * side, 2 - side, 3 - 3 * side
    my_mid, my_end = at(xi, z_mid), at(xi, z_end)
    far_mid, far_end = at(xi, z_far), at(xi, z_edge)
    line = jnp.where(mid, far_mid, my_mid)

    barrier = pltpu.get_barrier_semaphore()

    def greet(**where):
        pl.semaphore_signal(barrier, inc=1, device_id=where, device_id_type=pl.DeviceIdType.MESH)

    greet(dp=pal)

    @pl.when(mid)
    def _():
        greet(dp=far_mid)
        for e in range(groups):
            greet(dp=my_end, expert=e)
        for k in range(1, groups):
            greet(expert=lax.rem(mine + k, groups))

    local = [pltpu.make_async_copy(src, dst, l_sem.at[i]) for i, (src, dst) in enumerate((
        (gate_in.at[0], gate_buf.at[me]), (down_in.at[0], down_buf.at[me]),
        (ids_in, ids_v), (sc_in, sc_v), (tok_in, tok_v), (dout_in, dout_v)))]
    for c in local:
        c.start()
    pl.semaphore_wait(barrier, 1 + groups)

    def piece(s, p, way, own=False):
        if p < 4:
            part = pl.ds(p * (rows // 4), rows // 4)
            src = gate_buf.at[s, part]
            dst = gate_buf.at[s, part]
        else:
            part = pl.ds((p - 4) * (rows // 2), rows // 2)
            src = down_buf.at[s, part]
            dst = down_buf.at[s, part]
        return remote(src, dst, w_send.at[way, s, p], w_recv.at[s, p], dp=(line, pal)[way])

    def own_out(way, *ps):
        for p in ps:
            piece(me, p, way, True).start()

    def take(s, p, *out):
        piece(s, p, 0).wait_recv()
        for way in out:
            piece(s, p, way).start()

    for c in local[:2]:
        c.wait()
    for p in range(4):
        own_out(0, p)
        own_out(1, p)

    @pl.when(end)
    def _():
        for p in (4, 5):
            own_out(0, p)
            own_out(1, p)

    for c in local[2:]:
        c.wait()
    t_rows = tok_v.shape[0]
    topk = ids_v.shape[0]
    row = lax.broadcasted_iota(jnp.int32, (slots, t_rows), 0)
    row_e = row // PAD
    row_r = (row - row_e * PAD).astype(F32)
    idv = ids_v[...]
    scv = sc_v[...].astype(F32)
    live = jnp.zeros((slots, t_rows), F32)
    gcol = jnp.zeros((slots, t_rows), F32)
    hits = []
    for k in range(topk):
        hit = idv[k:k + 1, :] == row_e
        hits.append(hit)
        live = jnp.where(hit, 1.0, live)
        gcol = jnp.where(hit, scv[k:k + 1, :], gcol)
    upper = (lax.broadcasted_iota(jnp.int32, (t_rows, t_rows), 0)
             < lax.broadcasted_iota(jnp.int32, (t_rows, t_rows), 1))
    rank = dot(live.astype(BF), jnp.where(upper, 1.0, 0.0).astype(BF))
    pick_t = jnp.where(rank == row_r, live, 0.0)
    pick_b = pick_t.astype(BF)
    gate_col = jnp.sum(pick_t * gcol, axis=1, keepdims=True)

    def block(i):
        start = i * PAD
        return pl.ds(start if isinstance(i, int) else pl.multiple_of(start, PAD), PAD)

    outs, ins = (x_out, d_out), (x_in, d_in)
    quarter = feats // 4
    sent_cols = (pl.ds(0, 3 * quarter), pl.ds(0, LANES + 3 * quarter))

    def fold_in(kind, whole):
        base = kind * LANES
        behind = whole[:, 3 * quarter:]
        for j in range(FOLD):
            part = whole[:, j * quarter:(j + 1) * quarter].astype(F32) + dot(spread(groups, j, True), behind)
            outs[kind][:, base + j * quarter:base + (j + 1) * quarter] = part.astype(BF)

    def unfold(kind):
        base = kind * LANES
        tail = sum(dot(spread(2 * groups, j, False), ins[kind][:, base + j * quarter:base + (j + 1) * quarter])
                   for j in range(FOLD))
        ins[kind][:, base + 3 * quarter:base + feats] = tail.astype(BF)

    def slots_to(kind, e, place):
        return remote(outs[kind].at[block(e), :], ins[kind].at[block(place * groups + mine), sent_cols[kind]],
                      s_send.at[kind, e], s_recv.at[kind, place, mine], dp=my_mid, expert=e)

    def slots_from(kind, place, e):
        return remote(outs[kind].at[block(e), :], ins[kind].at[block(place * groups + e), sent_cols[kind]],
                      s_send.at[kind, e], s_recv.at[kind, place, e], dp=my_mid, expert=e)

    def other(k):
        return lax.rem(mine + k, groups)

    def slots_out(kind):
        @pl.when(end)
        def _():
            for e in range(groups):
                slots_to(kind, e, 1).start()

        @pl.when(mid)
        def _():
            for k in range(1, groups):
                slots_to(kind, other(k), 0).start()
            ins[kind][block(mine), sent_cols[kind]] = outs[kind][block(mine), :]

    fold_in(0, dot(pick_b, tok_v[...]).astype(BF))
    slots_out(0)
    d_out[:, :LANES] = jnp.broadcast_to(gate_col, (slots, LANES)).astype(BF)
    fold_in(1, (gate_col * dot(pick_b, dout_v[...])).astype(BF))

    @pl.when(end)
    def _():
        for p in range(4):
            take(pal, p, 0)

    slots_out(1)

    @pl.when(end)
    def _():
        for p in (4, 5):
            take(pal, p, 0)

    pick = jnp.transpose(pick_t).astype(BF)
    folded = [dot(pick, spread(groups, j, False)).astype(BF) for j in range(FOLD)]

    def dx_to(d):
        return remote(dx_send.at[d], dx_buf.at[2 * side + xi], x_send.at[d], x_recv.at[2 * side + xi], dp=d)

    def dx_from(q):
        return remote(dx_send.at[0], dx_buf.at[q], x_send.at[0], x_recv.at[q], dp=pal)

    def hid(q, d):
        return remote(hid_buf.at[q], hid_buf.at[q], h_send.at[q, d], h_recv.at[q], dp=d)

    rets, backs = (ret_a, ret_b), (back_a, back_b)

    def ret_to(part, place, e):
        return remote(rets[part].at[block(place * groups + e), :], backs[part].at[block(mine), :],
                      b_send.at[part, place, e], b_recv.at[part, mine], dp=(my_mid, my_end)[place], expert=e)

    def back_from(part, e):
        return remote(rets[part].at[block(e), :], backs[part].at[block(e), :],
                      b_send.at[part, 0, e], b_recv.at[part, e], dp=my_mid, expert=e)

    def ret_out(part):
        for e in range(groups):
            ret_to(part, 1, e).start()
        for k in range(1, groups):
            ret_to(part, 0, other(k)).start()
        backs[part][block(mine), :] = rets[part][block(mine), :]

    my_q, pal_q = 2 * side + xi, 2 * side + xo
    far_q, fpal_q = 2 - 2 * side + xi, 2 - 2 * side + xo
    a, b, c, d, e_, f, g = (my_end, at(xo, z_end), pal, far_mid, far_end, at(xo, z_far), at(xo, z_edge))

    @pl.when(mid)
    def _():
        many = 2 * slots
        packed = 2 * groups * CAP

        def cols(s, base=0):
            return pl.ds(pl.multiple_of(base + s * rows, LANES), rows)

        def add(s):
            pre_acc[...] += dot(x_in[:, cols(s)], gate_buf[s])

        def add_v(s):
            v_acc[...] += dot(d_in[:, cols(s, LANES)], down_buf[s])

        def slots_wait(kind):
            for k in range(1, groups):
                slots_from(kind, 0, other(k)).wait_recv()
            for e in range(groups):
                slots_from(kind, 1, e).wait_recv()
            unfold(kind)

        pr = lax.broadcasted_iota(jnp.int32, (packed, many), 0)
        pc = lax.broadcasted_iota(jnp.int32, (packed, many), 1)
        pack_v[...] = jnp.where(pc == (pr // CAP) * PAD + pr % CAP, 1.0, 0.0).astype(BF)
        for j in range(FOLD):
            spread_v[j] = spread(2 * groups, j, True)
        take(a, 0, 0)
        take(a, 1, 0)
        take(d, 2, 1)
        own_out(1, 4)
        take(a, 2, 0)
        take(d, 3, 1)
        take(a, 3, 0)
        take(c, 0, 0)
        take(c, 1, 0)
        own_out(0, 4, 5)
        take(a, 4, 0)
        take(a, 5, 0)
        for p in range(4):
            take(e_, p, 1)
        own_out(1, 5)
        slots_wait(0)
        pre_acc[...] = dot(x_in[:, cols(me)], gate_buf[me])
        take(c, 2)
        take(c, 3)
        take(d, 0)
        take(d, 1)
        for s in (a, c, d, e_):
            add(s)
        def rest(s):
            for p in range(4):
                take(s, p)
            add(s)

        rest(f)
        rest(g)
        rest(b)

        pre = pre_acc[...]
        ga = pre[:, :width]
        gb = pre[:, width:]
        sig = jax.nn.sigmoid(ga)
        act = ga * sig
        slope = gb * sig * (1.0 + ga * (1.0 - sig))
        hidden = (act * gb).astype(BF)
        hid_buf[my_q] = dot(pack_v[...], hidden).astype(BF)
        hid(my_q, my_end).start()
        hid(my_q, far_end).start()
        take(c, 4, 0)
        take(d, 5, 1)
        take(e_, 4, 1)
        take(e_, 5, 1)
        for s in (pal, far_mid):
            hid(my_q, s).start()

        slots_wait(1)
        dexp = dot(pack_v[...], d_in[:, LANES:]).astype(BF)
        for s in range(n):
            dx_send[s] = dexp[:, s * rows:(s + 1) * rows]
        for s in (e_, g, a, b):
            dx_to(s).start()
        dx_buf[my_q] = dx_send[me]
        gates = d_in[:, :1].astype(F32)
        inverse = jnp.where(gates > 0.0, 1.0 / jnp.where(gates > 0.0, gates, 1.0), 0.0)
        v_acc[...] = dot(d_in[:, cols(me, LANES)], down_buf[me])
        take(c, 5)
        take(d, 4)
        for s in (a, c, d, e_):
            add_v(s)
        for s in (f, b, g):
            take(s, 4)
            take(s, 5)
            add_v(s)

        used = lax.broadcasted_iota(jnp.int32, (many, width), 0) % PAD < CAP
        d_hid = jnp.where(used, v_acc[...], 0.0)
        d_pre = jnp.concatenate([d_hid * slope, d_hid * act], axis=1).astype(BF)
        quarter = feats // 4

        def d_slot(j):
            w = gate_buf[j * n // 4:(j + 1) * n // 4].reshape(quarter, 2 * width)
            return dot(d_pre, w, ((1,), (1,)))

        last = d_slot(3).astype(BF)

        def fold(j):
            return (d_slot(j) + dot(spread_v[j], last)).astype(BF)

        ret_a[...] = fold(0)
        ret_out(0)
        for j in range(1, FOLD):
            ret_b[:, (j - 1) * quarter:j * quarter] = fold(j)
        slot_grad = jnp.sum(hidden.astype(F32) * d_hid, axis=1, keepdims=True) * inverse
        ret_b[:, 2 * quarter:] = jnp.broadcast_to(slot_grad, (many, LANES)).astype(BF)
        ret_out(1)

        for s in (d, f, c):
            dx_to(s).start()
        hid(far_q, me).wait_recv()
        hid(far_q, pal).start()
        o_down[0] = dot(dx_buf[my_q], hid_buf[my_q], ((0,), (0,)))
        dx_from(far_q).wait_recv()
        o_down[0] += dot(dx_buf[far_q], hid_buf[far_q], ((0,), (0,)))

    @pl.when(end)
    def _():
        for q in (my_q, far_q):
            hid(q, me).wait_recv()
            hid(q, pal).start()
        dx_from(my_q).wait_recv()
        dx_from(far_q).wait_recv()
        o_down[0] = (dot(dx_buf[my_q], hid_buf[my_q], ((0,), (0,)))
                     + dot(dx_buf[far_q], hid_buf[far_q], ((0,), (0,))))

    def grow(q):
        hid(q, me).wait_recv()
        dx_from(q).wait_recv()
        o_down[0] += dot(dx_buf[q], hid_buf[q], ((0,), (0,)))

    grow(pal_q)
    quarter = feats // 4

    def back_wait(part):
        for k in range(1, groups):
            back_from(part, other(k)).wait_recv()
        pl.when(end)(lambda: back_from(part, mine).wait_recv())

    back_wait(0)
    o_tok[:, :quarter] = dot(pick, back_a[...]).astype(BF)
    last = dot(folded[0], back_a[...])
    grow(fpal_q)
    back_wait(1)
    for j in range(1, FOLD):
        part = back_b[:, (j - 1) * quarter:j * quarter]
        o_tok[:, j * quarter:(j + 1) * quarter] = dot(pick, part).astype(BF)
        last += dot(folded[j], part)
    o_tok[:, 3 * quarter:] = last.astype(BF)
    weighted = pick_t * back_b[:, 2 * quarter:2 * quarter + 1].astype(F32)
    o_gates[...] = jnp.concatenate(
        [jnp.sum(jnp.where(hit, weighted, 0.0), axis=0, keepdims=True) for hit in hits],
        axis=0).astype(BF)

    for p in range(6):
        for way in range(2):
            piece(me, p, way, True).wait_send()

    @pl.when(end)
    def _():
        for e in range(groups):
            slots_to(0, e, 1).wait_send()
            slots_to(1, e, 1).wait_send()
        for p in range(6):
            piece(pal, p, 0).wait_send()
        for q in (my_q, far_q):
            hid(q, pal).wait_send()

    @pl.when(mid)
    def _():
        for p in range(6):
            piece(a, p, 0).wait_send()
        for s, p, way in ((c, 0, 0), (c, 1, 0), (c, 4, 0), (d, 2, 1), (d, 3, 1), (d, 5, 1)):
            piece(s, p, way).wait_send()
        for p in range(6):
            piece(e_, p, 1).wait_send()
        for k in range(1, groups):
            slots_to(0, other(k), 0).wait_send()
            slots_to(1, other(k), 0).wait_send()
            for part in range(2):
                ret_to(part, 0, other(k)).wait_send()
        for e in range(groups):
            for part in range(2):
                ret_to(part, 1, e).wait_send()
        for s in (far_end, far_mid, my_end, pal):
            hid(my_q, s).wait_send()
        hid(far_q, pal).wait_send()
        for s in (a, b, c, d, e_, f, g):
            dx_to(s).wait_send()


def place(*refs):
    ins, outs, sem = refs[:3], refs[3:6], refs[6]
    copies = [pltpu.make_async_copy(src, dst, sem.at[i]) for i, (src, dst) in enumerate(zip(ins, outs))]
    for c in copies:
        c.start()
    for c in copies:
        c.wait()


def place_whole(*refs):
    for src, dst in zip(refs[:3], refs[3:]):
        dst[...] = src[...]


def solution(mesh):
    groups = mesh.shape["expert"]
    n = mesh.shape["dp"]
    inner = 1
    while n % (inner * 2) == 0 and (inner * 2) ** 2 <= n:
        inner *= 2
    outer = n // inner

    def on_device(tokens, d_output, expert_ids, gate_scores, gate_up_w, down_w):
        feats = tokens.shape[1]
        rows = gate_up_w.shape[1]
        width = down_w.shape[2]
        slots = groups * PAD
        packed = groups * CAP
        vmem = pl.BlockSpec(memory_space=pltpu.VMEM)
        dma = pltpu.SemaphoreType.DMA
        grads, d_gates, d_down = pl.pallas_call(
            functools.partial(ring_kernel, groups, outer, inner),
            out_shape=(
                jax.ShapeDtypeStruct(tokens.shape, BF),
                jax.ShapeDtypeStruct(gate_scores.shape[::-1], BF),
                jax.ShapeDtypeStruct(down_w.shape, F32),
            ),
            in_specs=[vmem] * 6,
            out_specs=(vmem,) * 3,
            scratch_shapes=[
                pltpu.VMEM((n, rows, 2 * width), BF),
                pltpu.VMEM((n, rows, width), BF),
                pltpu.VMEM((n, slots, rows), BF),
                pltpu.VMEM((n, slots, rows), BF),
                pltpu.VMEM((slots, 2 * width), F32),
                pltpu.VMEM((slots, width), F32),
                pltpu.VMEM((slots, 2 * feats + LANES), BF),
                pltpu.VMEM((slots, 2 * feats + LANES), BF),
                pltpu.VMEM((n, packed, width), BF),
                pltpu.VMEM((n, packed, rows), BF),
                pltpu.VMEM((n, packed, rows), BF),
                pltpu.VMEM((slots, feats + LANES), BF),
                pltpu.VMEM((slots, feats + LANES), BF),
                dma((2, 4, n)), dma((2, n)), dma((2,)),
                dma((groups,)), dma((groups,)),
                dma((n,)), dma((n,)),
                dma((n,)), dma((n,)),
                dma((groups,)), dma((groups,)),
            ],
            compiler_params=pltpu.CompilerParams(
                collective_id=0, has_side_effects=True, vmem_limit_bytes=60 * 2**20),
        )(tokens, d_output, expert_ids.T, gate_scores.T, gate_up_w, down_w)
        grads, d_gates, d_down = pl.pallas_call(
            place_whole,
            out_shape=tuple(jax.ShapeDtypeStruct(v.shape, v.dtype) for v in (grads, d_gates, d_down)),
            in_specs=[vmem] * 3,
            out_specs=(vmem,) * 3,
        )(grads, d_gates, d_down)
        return grads, d_gates.T, d_down

    def paired(tokens, d_output, expert_ids, gate_scores, gate_up_w, down_w):
        t_rows, feats = tokens.shape
        topk = expert_ids.shape[1]
        rows = gate_up_w.shape[1]
        width = down_w.shape[2]
        slots = groups * PAD
        packed = 2 * groups * CAP
        vmem = pl.BlockSpec(memory_space=pltpu.VMEM)
        hbm = pl.BlockSpec(memory_space=pltpu.HBM)
        dma = pltpu.SemaphoreType.DMA
        shapes = (
            jax.ShapeDtypeStruct(tokens.shape, BF),
            jax.ShapeDtypeStruct(gate_scores.shape[::-1], BF),
            jax.ShapeDtypeStruct(down_w.shape, F32),
        )
        parts = pl.pallas_call(
            functools.partial(mid_kernel, groups),
            out_shape=shapes,
            in_specs=[hbm] * 6,
            out_specs=(vmem,) * 3,
            scratch_shapes=[
                pltpu.VMEM((n, rows, 2 * width), BF),
                pltpu.VMEM((n, rows, width), BF),
                pltpu.VMEM((t_rows, feats), BF),
                pltpu.VMEM((t_rows, feats), BF),
                pltpu.VMEM((topk, t_rows), jnp.int32),
                pltpu.VMEM((topk, t_rows), BF),
                pltpu.VMEM((slots, feats // 4 * 3), BF),
                pltpu.VMEM((slots, feats // 4 * 3 + LANES), BF),
                pltpu.VMEM((2 * slots, feats), BF),
                pltpu.VMEM((2 * slots, feats + LANES), BF),
                pltpu.VMEM((2 * slots, 2 * width), F32),
                pltpu.VMEM((2 * slots, width), F32),
                pltpu.VMEM((n, packed, rows), BF),
                pltpu.VMEM((4, packed, rows), BF),
                pltpu.VMEM((4, packed, width), BF),
                pltpu.VMEM((2 * slots, feats // 4), BF),
                pltpu.VMEM((2 * slots, feats // 2 + LANES), BF),
                pltpu.VMEM((slots, feats // 4), BF),
                pltpu.VMEM((slots, feats // 2 + LANES), BF),
                pltpu.VMEM((packed, 2 * slots), BF),
                pltpu.VMEM((FOLD, 2 * slots, 2 * slots), BF),
                dma((6,)),
                dma((2, n, 6)), dma((n, 6)),
                dma((2, groups)), dma((2, 2, groups)),
                dma((n,)), dma((4,)),
                dma((4, n)), dma((4,)),
                dma((2, 2, groups)), dma((2, groups)),
            ],
            compiler_params=pltpu.CompilerParams(
                collective_id=0, has_side_effects=True, vmem_limit_bytes=16 * 2**20),
        )(*(pltpu.with_memory_space_constraint(v, pltpu.HBM) for v in (
            gate_up_w, down_w, tokens, d_output, expert_ids.T, gate_scores.T)))
        grads, d_gates, d_down = pl.pallas_call(
            place,
            out_shape=shapes,
            in_specs=[vmem] * 3,
            out_specs=(hbm,) * 3,
            scratch_shapes=[dma((3,))],
            compiler_params=pltpu.CompilerParams(vmem_limit_bytes=2**20),
        )(*parts)
        return grads, d_gates.T, d_down

    lines = inner == 2 and outer == 4
    tok = P(("expert", "dp"), None)
    w = P("expert", "dp", None)
    return jax.shard_map(
        paired if lines else on_device, mesh=mesh, in_specs=(tok, tok, tok, tok, w, w),
        out_specs=(tok, tok, w), check_vma=False)
```
